32 devices in a mesh: wide: 8 (over z, x), narrow: 4 (over y, core).
Axes of the slice: x: 2, y: 2, z: 4, core: 2. Of those that a mesh axis runs over, the one named last changes fastest.
Arguments:
- tokens: bfloat16 [1088, 8192], P('narrow', 'wide'), may hold values from -6 to 6
- cotangent: bfloat16 [1088, 8192], P('narrow', 'wide'), may hold values from -6 to 6
- segment_ids: int32 [8192], P('wide'), may hold values from 0 to 24, never falling along the last dimension, each value on 1 to 1000 neighbouring positions
- ln1_gain: float32 [1088], P('narrow'), may hold values from 0.25 to 1.75
- ln1_shift: float32 [1088], P('narrow'), may hold values from -1.75 to 1.75
- w_query: bfloat16 [1088, 1088], P('wide', 'narrow'), may hold values from -0.1875 to 0.1875
- w_key: bfloat16 [1088, 1088], P('wide', 'narrow'), may hold values from -0.1875 to 0.1875
- w_value: bfloat16 [1088, 1088], P('wide', 'narrow'), may hold values from -0.1875 to 0.1875
- bias_query: float32 [1088], P('narrow'), may hold values from -1.75 to 1.75
- bias_value: float32 [1088], P('narrow'), may hold values from -1.75 to 1.75
- w_out: bfloat16 [1088, 1088], P('wide', 'narrow'), may hold values from -0.5 to 0.5
- bias_out: float32 [1088], P('narrow'), may hold values from -1.75 to 1.75
- ln2_gain: float32 [1088], P('narrow'), may hold values from 0.25 to 1.75
- ln2_shift: float32 [1088], P('narrow'), may hold values from -1.75 to 1.75
- w_up: bfloat16 [1088, 4352], P('wide', 'narrow'), may hold values from -0.1875 to 0.1875
- bias_up: float32 [4352], P('narrow'), may hold values from -3 to 3
- w_down: bfloat16 [4352, 1088], P('wide', 'narrow'), may hold values from -0.09375 to 0.09375
- bias_down: float32 [1088], P('narrow'), may hold values from -1.75 to 1.75
Outputs:
- output: bfloat16 [1088, 8192], P('narrow', 'wide')
- grad_tokens: float32 [1088, 8192], P('narrow', 'wide')
- grad_ln1_gain: float32 [1088], P('narrow')
- grad_ln1_shift: float32 [1088], P('narrow')
- grad_w_query: float32 [1088, 1088], P('wide', 'narrow')
- grad_w_key: float32 [1088, 1088], P('wide', 'narrow')
- grad_w_value: float32 [1088, 1088], P('wide', 'narrow')
- grad_bias_query: float32 [1088], P('narrow')
- grad_bias_value: float32 [1088], P('narrow')
- grad_w_out: float32 [1088, 1088], P('wide', 'narrow')
- grad_bias_out: float32 [1088], P('narrow')
- grad_ln2_gain: float32 [1088], P('narrow')
- grad_ln2_shift: float32 [1088], P('narrow')
- grad_w_up: float32 [1088, 4352], P('wide', 'narrow')
- grad_bias_up: float32 [4352], P('narrow')
- grad_w_down: float32 [4352, 1088], P('wide', 'narrow')
- grad_bias_down: float32 [1088], P('narrow')
The draws below stay inside these ranges and needn't reach their ends.
Inputs may be any that keep to these rules, and one draw needn't show every extreme that they name: `segment_ids`: document numbers never fall along the tokens; a document has 1 to 1000 tokens, and one has exactly 1000.
All inputs are finite; a program needn't handle non-finite values.
Results may differ from the reference program's by a relative error of at most 0.014.
Values may be sent and summed in bfloat16 or wider, within the bound.
No kernel may reach another device: no remote copies, remote signals or barrier semaphores. Data moves between devices by JAX's collectives and lax.ppermute only.
A program may use at most 192 MiB of HBM per device.

```python
import math
import jax
import jax.numpy as jnp
import numpy as np
from jax import lax

D = 1088
HEADS = 17
HEAD_DIM = 64
FF = 4352
SEQ_LEN = 1024
DOC_MOST = 1000
TOKENS = 8192


def block_levels(stream_key, extent, pieces, low, largest):
    factor_of, own = 1.0, jax.random.fold_in(stream_key, 6)
    for dim, parts in pieces:
        heights = jnp.exp(jax.random.uniform(jax.random.fold_in(own, dim), (parts,), jnp.float32, low / len(pieces), largest / len(pieces)))
        factor_of = factor_of * jnp.repeat(heights, extent[dim] // parts).reshape([-1 if axis == dim else 1 for axis in range(len(extent))])
    return factor_of


def length_profile(count, total, limit, skew):
    portions = [(1 << 20) // math.isqrt(rank ** skew) + 1 for rank in range(2, count + 1)]
    rest, holding = total - limit - (count - 1), [1] * (count - 1)
    while rest > 0:
        movable = [i for i in range(count - 1) if holding[i] < limit]
        whole, budget = sum([portions[i] for i in movable]), rest
        for i in movable:
            more = min(limit - holding[i], max(1, budget * portions[i] // whole), rest)
            holding[i] = holding[i] + more
            rest = rest - more
    return np.array([limit] + holding)


def uneven_parts(rng, number_of, total, reach, lean):
    if number_of == 2:
        one = jax.random.randint(rng, (), max(1, total - reach), min(reach, total - 1) + 1)
        return jnp.stack([one, total - one])
    tallies = jnp.asarray(length_profile(number_of, total, reach, lean), jnp.int32)
    couples = (number_of - 1) // 2
    giver, taker = tallies[1:1 + 2 * couples:2], tallies[2:2 + 2 * couples:2]
    margin = jnp.minimum(giver - 1, reach - taker)
    passed = jax.random.randint(jax.random.fold_in(rng, 1), (couples,), 0, 1 << 20) % (margin + 1)
    tallies = tallies.at[1:1 + 2 * couples:2].set(giver - passed).at[2:2 + 2 * couples:2].set(taker + passed)
    return tallies[jax.random.permutation(jax.random.fold_in(rng, 2), number_of)]


def noise(rng, extent, deviation, most, pieces=(), held_as=jnp.bfloat16):
    values = deviation * jax.random.normal(rng, extent, jnp.float32)
    if pieces:
        values = values * block_levels(rng, extent, pieces, -0.22, 0.18)
    return jnp.clip(values, -most, most).astype(held_as)


def setup_inputs(seed: int = 0) -> dict:
    streams_of = jax.random.split(jax.random.key(seed), 19)
    tokens = noise(streams_of[0], (D, TOKENS), 1.0, 6.0, ((0, 4), (1, 8)))
    cotangent = noise(streams_of[1], (D, TOKENS), 1.0, 6.0, ((0, 4), (1, 8)))
    segment_ids = jnp.searchsorted(jnp.cumsum(uneven_parts(streams_of[2], TOKENS * 3 // DOC_MOST + 1, TOKENS, DOC_MOST, 1)), jnp.arange(TOKENS), side="right").astype(jnp.int32)
    ln1_gain = jnp.clip(1.0 + 0.15 * jax.random.normal(streams_of[3], (D,), jnp.float32), 0.25, 1.75)
    ln1_shift = noise(streams_of[4], (D,), 0.3, 1.75, ((0, 4),), jnp.float32)
    w_query = noise(streams_of[5], (D, D), D ** -0.5, 0.1875, ((0, 8), (1, 4)))
    w_key = noise(streams_of[6], (D, D), D ** -0.5, 0.1875, ((0, 8), (1, 4)))
    w_value = noise(streams_of[7], (D, D), D ** -0.5, 0.1875, ((0, 8), (1, 4)))
    bias_query = noise(streams_of[8], (D,), 0.3, 1.75, ((0, 4),), jnp.float32)
    bias_value = noise(streams_of[9], (D,), 0.3, 1.75, ((0, 4),), jnp.float32)
    w_out = noise(streams_of[10], (D, D), (D // 8) ** -0.5, 0.5, ((0, 8), (1, 4)))
    bias_out = noise(streams_of[11], (D,), 0.3, 1.75, ((0, 4),), jnp.float32)
    ln2_gain = jnp.clip(1.0 + 0.15 * jax.random.normal(streams_of[12], (D,), jnp.float32), 0.25, 1.75)
    ln2_shift = noise(streams_of[13], (D,), 0.3, 1.75, ((0, 4),), jnp.float32)
    w_up = noise(streams_of[14], (D, FF), D ** -0.5, 0.1875, ((0, 8), (1, 4)))
    bias_up = noise(streams_of[15], (FF,), 0.5, 3.0, ((0, 4),), jnp.float32)
    w_down = noise(streams_of[16], (FF, D), FF ** -0.5, 0.09375, ((0, 8), (1, 4)))
    bias_down = noise(streams_of[17], (D,), 0.3, 1.75, ((0, 4),), jnp.float32)
    return dict(tokens=tokens, cotangent=cotangent, segment_ids=segment_ids, ln1_gain=ln1_gain, ln1_shift=ln1_shift, w_query=w_query, w_key=w_key, w_value=w_value, bias_query=bias_query, bias_value=bias_value, w_out=w_out, bias_out=bias_out, ln2_gain=ln2_gain, ln2_shift=ln2_shift, w_up=w_up, bias_up=bias_up, w_down=w_down, bias_down=bias_down)


EPSILON = 1e-05

def matmul(left_side, right_side):
    return jnp.dot(left_side, right_side, preferred_element_type=jnp.float32)

def matmul_tleft(left_side, right_side):
    return jnp.dot(left_side.T, right_side, preferred_element_type=jnp.float32)

def matmul_tright(left_side, right_side):
    return jnp.dot(left_side, right_side.T, preferred_element_type=jnp.float32)

def layer_norm(inputs, norm_gain, norm_offset):
    row_mean = lax.optimization_barrier(jnp.mean(inputs, -1, keepdims=True))
    variance = lax.optimization_barrier(jnp.mean(inputs * inputs, -1, keepdims=True)) - row_mean * row_mean
    inv_std = lax.rsqrt(variance + EPSILON)
    centered = (inputs - row_mean) * inv_std
    return (centered, inv_std, centered * norm_gain + norm_offset)

def layer_norm_back(grad_normed, centered, inv_std, norm_gain):
    grad_centered = grad_normed * norm_gain
    return inv_std * (grad_centered - lax.optimization_barrier(jnp.mean(grad_centered, -1, keepdims=True)) - centered * lax.optimization_barrier(jnp.mean(grad_centered * centered, -1, keepdims=True)))

def gelu_tanh(values):
    return jax.nn.gelu(values, approximate=True)

def heads_of(matrix):
    return matrix.reshape(matrix.shape[0], HEADS, HEAD_DIM).astype(jnp.float32)

def reference(tokens, cotangent, segment_ids, ln1_gain, ln1_shift, w_query, w_key, w_value, bias_query, bias_value, w_out, bias_out, ln2_gain, ln2_shift, w_up, bias_up, w_down, bias_down):
    attn_scale = HEAD_DIM ** (-0.5)
    positions = jnp.arange(SEQ_LEN)

    def one_sequence(totals, sliced):
        seq_tokens, seq_cot, seq_segs = sliced
        inputs = seq_tokens.astype(jnp.float32)
        centered1, inv_std1, normed1 = layer_norm(inputs, ln1_gain, ln1_shift)
        normed1 = normed1.astype(jnp.bfloat16)
        query = (matmul(normed1, w_query) + bias_query).astype(jnp.bfloat16)
        keys = matmul(normed1, w_key).astype(jnp.bfloat16)
        values = (matmul(normed1, w_value) + bias_value).astype(jnp.bfloat16)
        query_h, key_h, value_h = (heads_of(query), heads_of(keys), heads_of(values))
        allowed = (seq_segs[:, None] == seq_segs[None, :]) & (positions[None, :] <= positions[:, None])
        scores = jnp.einsum('qhd,khd->hqk', query_h, key_h) * attn_scale
        masked = jnp.where(allowed[None], scores, -1e+30)
        top_score = lax.optimization_barrier(jnp.max(masked, -1))
        log_total = top_score + jnp.log(lax.optimization_barrier(jnp.sum(jnp.exp(masked - top_score[..., None]), -1)))
        probs = jnp.exp(masked - log_total[..., None])
        probs_b = probs.astype(jnp.bfloat16)
        attended = jnp.einsum('hqk,khd->qhd', probs_b.astype(jnp.float32), value_h)
        attended = attended.reshape(SEQ_LEN, D).astype(jnp.bfloat16)
        resid = inputs + matmul(attended, w_out) + bias_out
        centered2, inv_std2, normed2 = layer_norm(resid, ln2_gain, ln2_shift)
        normed2 = normed2.astype(jnp.bfloat16)
        hidden_pre = matmul(normed2, w_up) + bias_up
        hidden = gelu_tanh(hidden_pre).astype(jnp.bfloat16)
        output = (resid + matmul(hidden, w_down) + bias_down).astype(jnp.bfloat16)
        cot_float = seq_cot.astype(jnp.float32)
        grad_down = matmul_tleft(hidden, seq_cot)
        grad_bias_down = lax.optimization_barrier(jnp.sum(cot_float, 0))
        grad_hidden = matmul_tright(seq_cot, w_down)
        gelu_back = jax.vjp(gelu_tanh, hidden_pre)[1]
        grad_pre = gelu_back(grad_hidden)[0]
        grad_pre_b = grad_pre.astype(jnp.bfloat16)
        grad_up = matmul_tleft(normed2, grad_pre_b)
        grad_bias_up = lax.optimization_barrier(jnp.sum(grad_pre, 0))
        grad_normed2 = matmul_tright(grad_pre_b, w_up)
        grad_gain2 = lax.optimization_barrier(jnp.sum(grad_normed2 * centered2, 0))
        grad_shift2 = lax.optimization_barrier(jnp.sum(grad_normed2, 0))
        grad_resid = cot_float + layer_norm_back(grad_normed2, centered2, inv_std2, ln2_gain)
        grad_resid_b = grad_resid.astype(jnp.bfloat16)
        grad_wout = matmul_tleft(attended, grad_resid_b)
        grad_bias_out = lax.optimization_barrier(jnp.sum(grad_resid, 0))
        grad_attended = matmul_tright(grad_resid_b, w_out)
        grad_att_b = heads_of(grad_attended.astype(jnp.bfloat16))
        row_delta = lax.optimization_barrier(jnp.sum(grad_attended.reshape(SEQ_LEN, HEADS, HEAD_DIM) * heads_of(attended), -1)).T
        grad_probs = jnp.einsum('qhd,khd->hqk', grad_att_b, value_h)
        grad_scores = (probs * (grad_probs - row_delta[..., None])).astype(jnp.bfloat16).astype(jnp.float32)
        grad_query = (jnp.einsum('hqk,khd->qhd', grad_scores, key_h) * attn_scale).reshape(SEQ_LEN, D)
        grad_key = (jnp.einsum('hqk,qhd->khd', grad_scores, query_h) * attn_scale).reshape(SEQ_LEN, D)
        grad_value = jnp.einsum('hqk,qhd->khd', probs_b.astype(jnp.float32), grad_att_b).reshape(SEQ_LEN, D)
        query_b = grad_query.astype(jnp.bfloat16)
        key_b = grad_key.astype(jnp.bfloat16)
        value_b = grad_value.astype(jnp.bfloat16)
        grad_wq = matmul_tleft(normed1, query_b)
        grad_wk = matmul_tleft(normed1, key_b)
        grad_wv = matmul_tleft(normed1, value_b)
        grad_bq = lax.optimization_barrier(jnp.sum(grad_query, 0))
        grad_bv = lax.optimization_barrier(jnp.sum(grad_value, 0))
        grad_normed1 = matmul_tright(query_b, w_query) + matmul_tright(key_b, w_key) + matmul_tright(value_b, w_value)
        grad_gain1 = lax.optimization_barrier(jnp.sum(grad_normed1 * centered1, 0))
        grad_shift1 = lax.optimization_barrier(jnp.sum(grad_normed1, 0))
        grad_input = grad_resid + layer_norm_back(grad_normed1, centered1, inv_std1, ln1_gain)
        terms = (grad_gain1, grad_shift1, grad_wq, grad_wk, grad_wv, grad_bq, grad_bv, grad_wout, grad_bias_out, grad_gain2, grad_shift2, grad_up, grad_bias_up, grad_down, grad_bias_down)
        totals = tuple((total + term for total, term in zip(totals, terms)))
        return (totals, (output, grad_input))
    shapes = ((D,), (D,), (D, D), (D, D), (D, D), (D,), (D,), (D, D), (D,), (D,), (D,), (D, FF), (FF,), (FF, D), (D,))
    starting = tuple((jnp.zeros(shape, jnp.float32) for shape in shapes))
    sliced = (tokens.T.reshape(-1, SEQ_LEN, D), cotangent.T.reshape(-1, SEQ_LEN, D), segment_ids.reshape(-1, SEQ_LEN))
    totals, stacked = lax.scan(one_sequence, starting, sliced)
    output = stacked[0].reshape(-1, D).T
    grad_tokens = stacked[1].reshape(-1, D).T
    return (output, grad_tokens, totals[0], totals[1], totals[2], totals[3], totals[4], totals[5], totals[6], totals[7], totals[8], totals[9], totals[10], totals[11], totals[12], totals[13], totals[14])
```

```python
import functools

import jax
import jax.numpy as jnp
from jax import lax
from jax.experimental import pallas as pl
from jax.experimental.pallas import tpu as pltpu
from jax.sharding import PartitionSpec as P

D = 1088
HEADS = 17
HEAD_DIM = 64
SEQ_LEN = 1024
QUERY_BLOCK = 256
EPSILON = 1e-05
MASKED = -1e30
F32 = jnp.float32
BF16 = jnp.bfloat16


def dot(left_side, right_side, left_dim, right_dim):
    return lax.dot_general(
        left_side,
        right_side,
        (((left_dim,), (right_dim,)), ((), ())),
        preferred_element_type=F32,
    )


def gelu_tanh(values):
    return jax.nn.gelu(values, approximate=True)


def narrow_bits():
    count = lax.axis_size("narrow")
    return [1 << b for b in range(count.bit_length() - 1)]


def reverse_bits(value):
    bits = narrow_bits()
    last = len(bits) - 1
    return sum(((value >> k) & 1) << (last - k) for k in range(len(bits)))


def swap_narrow(value, mask):
    count = lax.axis_size("narrow")
    return lax.ppermute(value, "narrow", [(a, a ^ mask) for a in range(count)])


def narrow_pieces(block):
    held = {0: block}
    for bit in reversed(narrow_bits()):
        held.update({m ^ bit: swap_narrow(v, bit) for m, v in list(held.items())})
    return [held[reverse_bits(p)] for p in range(len(held))]


def in_order(pieces):
    index = lax.axis_index("narrow")
    by_mask = [pieces[reverse_bits(m)] for m in range(len(pieces))]
    return [lax.select_n(index ^ k, *by_mask) for k in range(len(pieces))]


def narrow_scatter(partial):
    current = partial
    for bit in narrow_bits():
        half = current.shape[0] // 2
        came = swap_narrow(current[half:].astype(BF16), bit)
        current = current[:half] + came.astype(F32)
    return current


def narrow_total(value):
    for bit in narrow_bits():
        value = value + swap_narrow(value, bit)
    return value


def narrow_exchange(blocks):
    return [
        swap_narrow(block, reverse_bits(p)) if p else block for p, block in enumerate(blocks)
    ]


def ring_place(device, count):
    return (device >> 1) ^ ((device & 1) * (count - 1))


def ring_device(place, count):
    return jnp.where(place < count // 2, 2 * place, 2 * (count - 1 - place) + 1)


def ring_step(value, direction):
    count = lax.axis_size("wide")
    order = list(range(0, count, 2)) + list(range(count - 1, 0, -2))
    return lax.ppermute(
        value, "wide", [(order[k], order[(k + direction) % count]) for k in range(count)]
    )


def feature_place(device):
    each = lax.axis_size("wide") // lax.axis_size("narrow")
    block = device >> (each.bit_length() - 1)
    return reverse_bits(block ^ lax.axis_index("narrow")) * each + (device & (each - 1))


def place_kernel(where_ref, *refs):
    pieces, out_ref, sems = refs[:-2], refs[-2], refs[-1]
    copies = [
        pltpu.make_async_copy(piece, out_ref.at[where_ref[k]], sems.at[k])
        for k, piece in enumerate(pieces)
    ]
    for copy in copies:
        copy.start()
    for copy in copies:
        copy.wait()


def wide_gather(block, place_of):
    count = lax.axis_size("wide")
    cut = block.shape[0] // 16 * 8
    pieces, hops = [block], [0]
    ahead = behind = block
    for hop in range(1, count // 2):
        ahead, behind = ring_step(ahead, 1), ring_step(behind, -1)
        pieces += [ahead, behind]
        hops += [-hop, hop]
    far = jnp.concatenate([ring_step(ahead[:cut], 1), ring_step(behind[cut:], -1)], 0)
    pieces.append(far)
    hops.append(count // 2)
    here = ring_place(lax.axis_index("wide"), count)
    places = place_of(ring_device((here + jnp.array(hops)) & (count - 1), count))
    whole = pl.pallas_call(
        place_kernel,
        grid_spec=pltpu.PrefetchScalarGridSpec(
            num_scalar_prefetch=1,
            grid=(1,),
            in_specs=[pl.BlockSpec(memory_space=pl.ANY)] * count,
            out_specs=pl.BlockSpec(memory_space=pl.ANY),
            scratch_shapes=[pltpu.SemaphoreType.DMA((count,))],
        ),
        out_shape=jax.ShapeDtypeStruct((count, *block.shape), block.dtype),
        name="place_blocks",
    )(places.astype(jnp.int32), *pieces)
    return whole.reshape(count * block.shape[0], block.shape[1]), pieces


def wide_scatter(partial, direction, place_of):
    count = lax.axis_size("wide")
    here = ring_place(lax.axis_index("wide"), count)

    def part(back):
        where = place_of(ring_device((here - direction * back) & (count - 1), count))
        return lax.dynamic_index_in_dim(partial, where, 0, keepdims=False)

    moving = part(1).astype(BF16)
    for hop in range(1, count):
        came = ring_step(moving, direction)
        moving = (came.astype(F32) + part(hop + 1).astype(F32)).astype(BF16)
    return moving


def wide_total(value):
    count = lax.axis_size("wide")
    bit = 1
    while bit < count:
        value = value + lax.ppermute(value, "wide", [(a, a ^ bit) for a in range(count)])
        bit *= 2
    return value


def turn_pairs(turn):
    wide, narrow = lax.axis_size("wide"), lax.axis_size("narrow")
    each = wide // narrow
    return [
        (each * b + h, narrow * h + (b + turn) % narrow)
        for b in range(narrow)
        for h in range(each)
    ]


def rows_to_blocks(shard):
    wide, narrow = lax.axis_size("wide"), lax.axis_size("narrow")
    device, index = lax.axis_index("wide"), lax.axis_index("narrow")
    block = device >> ((wide // narrow).bit_length() - 1)
    rows = shard.shape[0] // narrow
    came = []
    for turn in range(narrow):
        start = ((block + turn) & (narrow - 1)) * rows
        leaving = lax.dynamic_slice_in_dim(shard, start, rows, 0)
        came.append(lax.ppermute(leaving, "wide", turn_pairs(turn)))
    return [
        lax.select_n((device - (index ^ reverse_bits(p))) & (narrow - 1), *came)
        for p in range(narrow)
    ]


def blocks_to_rows(parts):
    wide, narrow = lax.axis_size("wide"), lax.axis_size("narrow")
    device, index = lax.axis_index("wide"), lax.axis_index("narrow")
    block = device >> ((wide // narrow).bit_length() - 1)
    came = []
    for turn in range(narrow):
        pairs = [(b, a) for a, b in turn_pairs(turn)]
        leaving = lax.select_n(
            reverse_bits(((device - turn) & (narrow - 1)) ^ index), *parts
        )
        came.append(lax.ppermute(leaving, "wide", pairs))
    return jnp.concatenate(
        [lax.select_n((k - block) & (narrow - 1), *came) for k in range(narrow)], 0
    )


def after(value, *others):
    return lax.optimization_barrier((value, *others))[0]


def scores_of(keys, query, starts, begin, extent):
    scores = dot(keys[0:extent, :], query * HEAD_DIM ** (-0.5), 1, 0)
    key_pos = lax.broadcasted_iota(jnp.int32, scores.shape, 0)
    query_pos = begin + lax.broadcasted_iota(jnp.int32, scores.shape, 1)
    return jnp.where((key_pos >= starts) & (key_pos <= query_pos), scores, MASKED)


def attend_kernel(query_ref, key_ref, value_ref, start_ref, out_ref, log_ref, keys):
    keys[...] = key_ref[...].T
    tokens = query_ref.shape[1]
    for begin in range(0, tokens, QUERY_BLOCK):
        extent = begin + QUERY_BLOCK
        span = slice(begin, extent)
        masked = scores_of(keys, query_ref[:, span], start_ref[:, span], begin, extent)
        top = jnp.max(masked, 0, keepdims=True)
        powers = jnp.exp(masked - top)
        total = jnp.sum(powers, 0, keepdims=True)
        log_total = top + jnp.log(total)
        probs = (powers * (1.0 / total)).astype(BF16)
        out_ref[:, span] = dot(value_ref[:, 0:extent], probs, 1, 0).astype(BF16)
        log_ref[0, :, span] = log_total


def attend(qkv, starts):
    heads, tokens = qkv.shape[0] // (3 * HEAD_DIM), qkv.shape[1]

    def piece(offset):
        return pl.BlockSpec((HEAD_DIM, tokens), lambda h: (offset * heads + h, 0))

    return pl.pallas_call(
        attend_kernel,
        grid=(heads,),
        in_specs=[piece(0), piece(1), piece(2), pl.BlockSpec((1, tokens), lambda h: (0, 0))],
        out_specs=[
            pl.BlockSpec((HEAD_DIM, tokens), lambda h: (h, 0)),
            pl.BlockSpec((1, 1, tokens), lambda h: (h, 0, 0)),
        ],
        out_shape=[
            jax.ShapeDtypeStruct((heads * HEAD_DIM, tokens), BF16),
            jax.ShapeDtypeStruct((heads, 1, tokens), F32),
        ],
        scratch_shapes=[pltpu.VMEM((tokens, HEAD_DIM), BF16)],
        name="attend",
    )(qkv, qkv, qkv, starts)


def attend_back_kernel(
    query_ref, key_ref, value_ref, start_ref, log_ref, grad_ref, out_ref,
    back_ref, sums_ref, keys, values, grad_keys, grad_values,
):
    scale = HEAD_DIM ** (-0.5)
    keys[...] = key_ref[...].T
    values[...] = value_ref[...].T
    tokens = query_ref.shape[1]
    grad_keys[...] = jnp.zeros_like(grad_keys)
    grad_values[...] = jnp.zeros_like(grad_values)
    query_sum = jnp.zeros((HEAD_DIM, 1), F32)
    for begin in range(0, tokens, QUERY_BLOCK):
        extent = begin + QUERY_BLOCK
        span = slice(begin, extent)
        query = query_ref[:, span]
        grad = grad_ref[:, span]
        grad_b = grad.astype(BF16)
        delta = jnp.sum(grad * out_ref[:, span].astype(F32), 0, keepdims=True)
        masked = scores_of(keys, query, start_ref[:, span], begin, extent)
        probs = jnp.exp(masked - log_ref[0, :, span])
        grad_probs = dot(values[0:extent, :], grad_b, 1, 0)
        grad_scores = (probs * (grad_probs - delta)).astype(BF16)
        grad_query = dot(key_ref[:, 0:extent], grad_scores, 1, 0) * scale
        query_sum += jnp.sum(grad_query, 1, keepdims=True)
        back_ref[0, :, span] = grad_query.astype(BF16)
        grad_keys[:, 0:extent] += dot(query, grad_scores, 1, 1)
        grad_values[:, 0:extent] += dot(grad_b, probs.astype(BF16), 1, 1)
    grad_value = grad_values[...]
    back_ref[1] = (grad_keys[...] * scale).astype(BF16)
    back_ref[2] = grad_value.astype(BF16)
    sums_ref[0] = jnp.broadcast_to(query_sum, sums_ref.shape[1:])
    sums_ref[1] = jnp.broadcast_to(
        jnp.sum(grad_value, 1, keepdims=True), sums_ref.shape[1:]
    )


def attend_back(qkv, starts, log_total, grad_attended, attended):
    heads, tokens = qkv.shape[0] // (3 * HEAD_DIM), qkv.shape[1]

    def piece(offset):
        return pl.BlockSpec((HEAD_DIM, tokens), lambda h: (offset * heads + h, 0))

    back, sums = pl.pallas_call(
        attend_back_kernel,
        grid=(heads,),
        in_specs=[
            piece(0), piece(1), piece(2),
            pl.BlockSpec((1, tokens), lambda h: (0, 0)),
            pl.BlockSpec((1, 1, tokens), lambda h: (h, 0, 0)),
            piece(0), piece(0),
        ],
        out_specs=[
            pl.BlockSpec((3, HEAD_DIM, tokens), lambda h: (0, h, 0)),
            pl.BlockSpec((2, HEAD_DIM, 128), lambda h: (0, h, 0)),
        ],
        out_shape=[
            jax.ShapeDtypeStruct((3, heads * HEAD_DIM, tokens), BF16),
            jax.ShapeDtypeStruct((2, heads * HEAD_DIM, 128), F32),
        ],
        scratch_shapes=[
            pltpu.VMEM((tokens, HEAD_DIM), BF16),
            pltpu.VMEM((tokens, HEAD_DIM), BF16),
            pltpu.VMEM((HEAD_DIM, tokens), F32),
            pltpu.VMEM((HEAD_DIM, tokens), F32),
        ],
        name="attend_back",
    )(qkv, qkv, qkv, starts, log_total, grad_attended, attended)
    return back.reshape(3 * heads * HEAD_DIM, tokens), sums[:, :, 0]


def norm_stats(inputs):
    mean = jnp.sum(inputs, 0) / D
    variance = jnp.sum(inputs * inputs, 0) / D - mean * mean
    return mean, lax.rsqrt(variance + EPSILON)


def center(inputs, stats):
    return (inputs - stats[0][None]) * stats[1][None]


def norm_back_sums(grad_normed, centered, gain):
    weighted = grad_normed * gain[:, None]
    return jnp.stack([jnp.sum(weighted, 0), jnp.sum(weighted * centered, 0)])


def norm_back(grad_normed, centered, inv_std, gain, sums):
    return inv_std[None] * (
        grad_normed * gain[:, None] - sums[0][None] / D - centered * (sums[1][None] / D)
    )


def per_device(
    tokens,
    cotangent,
    segment_ids,
    ln1_gain,
    ln1_shift,
    w_query,
    w_key,
    w_value,
    bias_query,
    bias_value,
    w_out,
    bias_out,
    ln2_gain,
    ln2_shift,
    w_up,
    bias_up,
    w_down,
    bias_down,
):
    narrow, wide = lax.axis_size("narrow"), lax.axis_size("wide")
    index = lax.axis_index("narrow")
    feats, toks = tokens.shape
    shard_rows = w_query.shape[0]
    own_cols = (HEADS - 1) // narrow * HEAD_DIM
    head_cols = own_cols + HEAD_DIM
    last = (HEADS - 1) * HEAD_DIM

    qkv_pieces = narrow_pieces(jnp.concatenate([w_query, w_key, w_value], 0))
    inputs = jnp.concatenate(narrow_pieces(tokens), 0)
    vectors = [ln1_gain, ln1_shift, bias_out, ln2_gain, ln2_shift, bias_query, bias_value]
    small = narrow_pieces(jnp.concatenate(vectors))

    def vector(k, pieces):
        return jnp.concatenate([piece[k * feats : (k + 1) * feats] for piece in pieces])

    gain1, shift1, bias_o, gain2, shift2 = [vector(k, small) for k in range(5)]
    small_ordered = in_order(small)
    bias_q, bias_v = vector(5, small_ordered), vector(6, small_ordered)
    qkv_rows = jnp.concatenate(in_order(qkv_pieces), 1)

    def heads_of(array):
        own = lax.dynamic_slice_in_dim(array, index * own_cols, own_cols, array.ndim - 1)
        return jnp.concatenate([own, array[..., last:]], -1)

    head_rows = heads_of(qkv_rows)
    attention_shard = jnp.concatenate(
        [head_rows[k * shard_rows : (k + 1) * shard_rows] for k in range(3)] + [w_out], 1
    )

    attention_cols, hops = wide_gather(attention_shard, feature_place)
    w_qkv = attention_cols[:, : 3 * head_cols]
    out_cols = attention_cols[:, 3 * head_cols :]
    down_shard = jnp.concatenate(
        narrow_exchange(rows_to_blocks(after(w_down, hops[2]))), 1
    )
    up_cols, hops = wide_gather(after(w_up, hops[-1]), feature_place)
    down_block, _ = wide_gather(after(down_shard, hops[-2]), lambda device: device)
    cot_full = jnp.concatenate(narrow_pieces(after(cotangent, hops[1])), 0)

    out_rows = in_order([out_cols[k * feats : (k + 1) * feats] for k in range(narrow)])
    out_full = jnp.concatenate(narrow_pieces(jnp.concatenate(out_rows, 0)), 1)

    rows_f = inputs.astype(F32)
    stats1 = norm_stats(rows_f)
    centered1 = center(rows_f, stats1)
    normed1 = (centered1 * gain1[:, None] + shift1[:, None]).astype(BF16)
    bias_qkv = jnp.concatenate(
        [heads_of(bias_q), jnp.zeros((head_cols,), F32), heads_of(bias_v)]
    )
    qkv = (dot(w_qkv, normed1, 0, 0) + bias_qkv[:, None]).astype(BF16)
    starts = jnp.sum(
        (segment_ids[:, None] < segment_ids[None, :]).astype(jnp.int32), 0, keepdims=True
    )
    attended, log_total = attend(qkv, starts)
    attended_full = jnp.concatenate(
        in_order(narrow_pieces(attended[:own_cols])) + [attended[own_cols:]], 0
    )
    resid = rows_f + dot(out_full, attended_full, 0, 0) + bias_o[:, None]

    stats2 = norm_stats(resid)
    centered2 = center(resid, stats2)
    normed2 = (centered2 * gain2[:, None] + shift2[:, None]).astype(BF16)
    hidden_pre = dot(up_cols, normed2, 0, 0) + bias_up[:, None]
    hidden, gelu_back = jax.vjp(gelu_tanh, hidden_pre)
    hidden = hidden.astype(BF16)
    grad_hidden = dot(down_block, cot_full, 1, 0)
    grad_pre = gelu_back(grad_hidden)[0]
    grad_pre_b = grad_pre.astype(BF16)
    grad_normed2 = dot(up_cols, grad_pre_b, 1, 0)
    sums2 = narrow_total(norm_back_sums(grad_normed2, centered2, gain2))
    grad_normed2_own = narrow_scatter(grad_normed2)

    resid_own = resid[:feats]
    output = (
        resid_own + (narrow_scatter(dot(down_block, hidden, 0, 0)) + bias_down[:, None])
    ).astype(BF16)
    grad_up = dot(normed2, grad_pre_b, 1, 1).astype(BF16)
    grad_down = dot(hidden, cot_full, 1, 1).astype(BF16)
    sum_up = wide_scatter(grad_up.reshape(wide, shard_rows, -1), 1, feature_place)
    sum_down = wide_scatter(grad_down.reshape(wide, -1, D), -1, lambda device: device)
    sum_down = blocks_to_rows(
        narrow_exchange([sum_down[:, k * feats : (k + 1) * feats] for k in range(narrow)])
    )

    cot_own = cotangent.astype(F32)
    centered2_own = center(resid_own, stats2)
    grad_resid = cot_own + norm_back(
        grad_normed2_own, centered2_own, stats2[1], ln2_gain, sums2
    )
    grad_resid_own = grad_resid.astype(BF16)
    grad_resid_b = jnp.concatenate(narrow_pieces(grad_resid_own), 0)

    out_heads = jnp.concatenate(
        [lax.dynamic_slice_in_dim(out_full, index * own_cols, own_cols, 0), out_full[last:]], 0
    )
    grad_attended = dot(out_heads, grad_resid_b, 1, 0)
    grad_qkv, head_sums = attend_back(qkv, starts, log_total, grad_attended, attended)
    grad_wout = dot(attended_full, grad_resid_own, 1, 1).astype(BF16)
    sum_wo = lax.psum_scatter(grad_wout, "wide", scatter_dimension=0, tiled=True)
    keep_last = (index == narrow - 1).astype(BF16)
    row_ids = jnp.arange(3 * head_cols) % head_cols
    counted = jnp.where(row_ids < own_cols, jnp.ones((), BF16), keep_last)
    half = (3 * head_cols + 128) // 256 * 128
    sum_qkv = jnp.concatenate(
        [
            wide_scatter(
                dot(normed1, grad, 1, 1).astype(BF16).reshape(wide, shard_rows, -1),
                direction,
                feature_place,
            )
            for grad, direction in ((grad_qkv[:half], 1), (grad_qkv[half:], -1))
        ],
        -1,
    )
    grad_normed1 = dot(w_qkv, grad_qkv * counted[:, None], 1, 0)
    sums1 = narrow_total(norm_back_sums(grad_normed1, centered1, gain1))
    grad_normed1_own = narrow_scatter(grad_normed1)
    sum_heads = jnp.concatenate(
        [sum_qkv[:, k * head_cols : (k + 1) * head_cols] for k in range(3)], 0
    )
    sum_cols = jnp.concatenate(
        in_order(narrow_pieces(sum_heads[:, :own_cols])) + [sum_heads[:, own_cols:]], 1
    )
    sum_own = lax.select_n(
        index, *[sum_cols[:, k * feats : (k + 1) * feats] for k in range(narrow)]
    ).astype(F32)

    centered1_own = center(tokens.astype(F32), stats1)
    grad_tokens = grad_resid + norm_back(
        grad_normed1_own, centered1_own, stats1[1], ln1_gain, sums1
    )

    placed = lax.dynamic_update_slice_in_dim(
        jnp.zeros((2, D), F32), head_sums[:, :own_cols], index * own_cols, 1
    )
    tail = jnp.where(index == narrow - 1, head_sums[:, own_cols:], 0.0)
    placed = lax.dynamic_update_slice_in_dim(placed, tail, last, 1)
    head_total = lax.dynamic_slice_in_dim(narrow_total(placed), index * feats, feats, 1)
    pieces = [
        jnp.sum(grad_normed1_own * centered1_own, 1),
        jnp.sum(grad_normed1_own, 1),
        head_total[0],
        head_total[1],
        jnp.sum(grad_resid, 1),
        jnp.sum(grad_normed2_own * centered2_own, 1),
        jnp.sum(grad_normed2_own, 1),
        jnp.sum(cot_own, 1),
        jnp.sum(grad_pre, 1),
    ]
    total = wide_total(jnp.concatenate(pieces))
    sums = [total[k * feats : (k + 1) * feats] for k in range(8)]
    return (
        output,
        grad_tokens,
        sums[0],
        sums[1],
        sum_own[:shard_rows],
        sum_own[shard_rows : 2 * shard_rows],
        sum_own[2 * shard_rows :],
        sums[2],
        sums[3],
        sum_wo.astype(F32),
        sums[4],
        sums[5],
        sums[6],
        sum_up.astype(F32),
        total[8 * feats :],
        sum_down.astype(F32),
        sums[7],
    )


def solution(mesh):
    matrix, vector = P("wide", "narrow"), P("narrow")
    acts = P("narrow", "wide")
    return jax.shard_map(
        per_device,
        mesh=mesh,
        in_specs=(
            acts, acts, P("wide"), vector, vector, matrix, matrix, matrix, vector, vector,
            matrix, vector, vector, vector, matrix, vector, matrix, vector,
        ),
        out_specs=(
            acts, acts, vector, vector, matrix, matrix, matrix, vector, vector,
            matrix, vector, vector, vector, matrix, vector, matrix, vector,
        ),
        check_vma=False,
    )
```

```python
import functools

import jax
import jax.numpy as jnp
from jax import lax
from jax.experimental import pallas as pl
from jax.experimental.pallas import tpu as pltpu
from jax.sharding import PartitionSpec as P

D = 1088
HEADS = 17
HEAD_DIM = 64
SEQ_LEN = 1024
QUERY_BLOCK = 256
EPSILON = 1e-05
MASKED = -1e30
F32 = jnp.float32
BF16 = jnp.bfloat16


def dot(left_side, right_side, left_dim, right_dim):
    return lax.dot_general(
        left_side,
        right_side,
        (((left_dim,), (right_dim,)), ((), ())),
        preferred_element_type=F32,
    )


def gelu_tanh(values):
    return jax.nn.gelu(values, approximate=True)


def narrow_bits():
    count = lax.axis_size("narrow")
    return [1 << b for b in range(count.bit_length() - 1)]


def reverse_bits(value):
    bits = narrow_bits()
    last = len(bits) - 1
    return sum(((value >> k) & 1) << (last - k) for k in range(len(bits)))


def swap_narrow(value, mask):
    count = lax.axis_size("narrow")
    return lax.ppermute(value, "narrow", [(a, a ^ mask) for a in range(count)])


def narrow_pieces(block):
    held = {0: block}
    for bit in reversed(narrow_bits()):
        held.update({m ^ bit: swap_narrow(v, bit) for m, v in list(held.items())})
    return [held[reverse_bits(p)] for p in range(len(held))]


def in_order(pieces):
    index = lax.axis_index("narrow")
    by_mask = [pieces[reverse_bits(m)] for m in range(len(pieces))]
    return [lax.select_n(index ^ k, *by_mask) for k in range(len(pieces))]


def narrow_scatter(partial):
    return narrow_stages(partial)[-1]


def narrow_stages(partial):
    stages = [partial]
    for bit in narrow_bits():
        half = stages[-1].shape[0] // 2
        came = swap_narrow(stages[-1][half:].astype(BF16), bit)
        stages.append(stages[-1][:half] + came.astype(F32))
    return stages


def narrow_total(value):
    for bit in narrow_bits():
        value = value + swap_narrow(value, bit)
    return value


def narrow_exchange(blocks):
    return [
        swap_narrow(block, reverse_bits(p)) if p else block for p, block in enumerate(blocks)
    ]


def ring_place(device, count):
    return (device >> 1) ^ ((device & 1) * (count - 1))


def ring_device(place, count):
    return jnp.where(place < count // 2, 2 * place, 2 * (count - 1 - place) + 1)


def ring_step(value, direction):
    count = lax.axis_size("wide")
    order = list(range(0, count, 2)) + list(range(count - 1, 0, -2))
    return lax.ppermute(
        value, "wide", [(order[k], order[(k + direction) % count]) for k in range(count)]
    )


def feature_place(device):
    each = lax.axis_size("wide") // lax.axis_size("narrow")
    block = device >> (each.bit_length() - 1)
    return reverse_bits(block ^ lax.axis_index("narrow")) * each + (device & (each - 1))


def place_kernel(where_ref, *refs, count):
    pieces, outs = refs[:count], refs[count:]
    for k, piece in enumerate(pieces):
        begin = 0
        for part, out_ref in enumerate(outs):
            cols = out_ref.shape[2]
            out_ref[where_ref[part, k]] = piece[:, begin : begin + cols]
            begin += cols


def wide_gather(block, parts):
    count = lax.axis_size("wide")
    cut = block.shape[0] // 16 * 8
    pieces, hops = [block], [0]
    ahead = behind = block
    for hop in range(1, count // 2):
        ahead, behind = ring_step(ahead, 1), ring_step(behind, -1)
        pieces += [ahead, behind]
        hops += [-hop, hop]
    far = jnp.concatenate([ring_step(ahead[:cut], 1), ring_step(behind[cut:], -1)], 0)
    pieces.append(far)
    hops.append(count // 2)
    here = ring_place(lax.axis_index("wide"), count)
    devices = ring_device((here + jnp.array(hops)) & (count - 1), count)
    places = jnp.stack([place_of(devices) for _, place_of in parts]).astype(jnp.int32)
    rows = block.shape[0]
    wholes = pl.pallas_call(
        functools.partial(place_kernel, count=count),
        grid_spec=pltpu.PrefetchScalarGridSpec(
            num_scalar_prefetch=1,
            grid=(1,),
            in_specs=[pl.BlockSpec(block.shape, lambda i, w: (0, 0))] * count,
            out_specs=[
                pl.BlockSpec((count, rows, width), lambda i, w: (0, 0, 0)) for width, _ in parts
            ],
        ),
        out_shape=[
            jax.ShapeDtypeStruct((count, rows, width), block.dtype) for width, _ in parts
        ],
        name="place_blocks",
    )(places, *pieces)
    return [whole.reshape(count * rows, whole.shape[2]) for whole in wholes], pieces


def wide_scatter(partials, direction, waits):
    count = lax.axis_size("wide")
    here = ring_place(lax.axis_index("wide"), count)

    def part(back):
        device = ring_device((here - direction * back) & (count - 1), count)
        return jnp.concatenate(
            [
                lax.dynamic_index_in_dim(partial, place_of(device), 0, keepdims=False)
                for partial, place_of in partials
            ],
            -1,
        )

    moving = part(1).astype(BF16)
    for hop in range(1, count):
        if hop in waits:
            moving = after(moving, waits[hop])
        came = ring_step(moving, direction)
        moving = (came.astype(F32) + part(hop + 1).astype(F32)).astype(BF16)
    return moving


def wide_total(value):
    count = lax.axis_size("wide")
    bit = 1
    while bit < count:
        value = value + lax.ppermute(value, "wide", [(a, a ^ bit) for a in range(count)])
        bit *= 2
    return value


def turn_pairs(turn):
    wide, narrow = lax.axis_size("wide"), lax.axis_size("narrow")
    each = wide // narrow
    return [
        (each * b + h, narrow * h + (b + turn) % narrow)
        for b in range(narrow)
        for h in range(each)
    ]


def rows_to_blocks(shard):
    wide, narrow = lax.axis_size("wide"), lax.axis_size("narrow")
    device, index = lax.axis_index("wide"), lax.axis_index("narrow")
    block = device >> ((wide // narrow).bit_length() - 1)
    rows = shard.shape[0] // narrow
    came = []
    for turn in range(narrow):
        start = ((block + turn) & (narrow - 1)) * rows
        leaving = lax.dynamic_slice_in_dim(shard, start, rows, 0)
        came.append(lax.ppermute(leaving, "wide", turn_pairs(turn)))
    return [
        lax.select_n((device - (index ^ reverse_bits(p))) & (narrow - 1), *came)
        for p in range(narrow)
    ]


def blocks_to_rows(parts):
    wide, narrow = lax.axis_size("wide"), lax.axis_size("narrow")
    device, index = lax.axis_index("wide"), lax.axis_index("narrow")
    block = device >> ((wide // narrow).bit_length() - 1)
    came = []
    for turn in range(narrow):
        pairs = [(b, a) for a, b in turn_pairs(turn)]
        leaving = lax.select_n(
            reverse_bits(((device - turn) & (narrow - 1)) ^ index), *parts
        )
        came.append(lax.ppermute(leaving, "wide", pairs))
    return jnp.concatenate(
        [lax.select_n((k - block) & (narrow - 1), *came) for k in range(narrow)], 0
    )


def after(value, *others):
    return lax.optimization_barrier((value, *others))[0]


def scores_of(keys, query, starts, begin, extent):
    scores = dot(keys[0:extent, :], query * HEAD_DIM ** (-0.5), 1, 0)
    key_pos = lax.broadcasted_iota(jnp.int32, scores.shape, 0)
    query_pos = begin + lax.broadcasted_iota(jnp.int32, scores.shape, 1)
    return jnp.where((key_pos >= starts) & (key_pos <= query_pos), scores, MASKED)


def attend_kernel(query_ref, key_ref, value_ref, start_ref, out_ref, log_ref, keys):
    keys[...] = key_ref[...].T
    tokens = query_ref.shape[1]
    for begin in range(0, tokens, QUERY_BLOCK):
        extent = begin + QUERY_BLOCK
        span = slice(begin, extent)
        masked = scores_of(keys, query_ref[:, span], start_ref[:, span], begin, extent)
        top = jnp.max(masked, 0, keepdims=True)
        powers = jnp.exp(masked - top)
        total = jnp.sum(powers, 0, keepdims=True)
        log_total = top + jnp.log(total)
        probs = (powers * (1.0 / total)).astype(BF16)
        out_ref[:, span] = dot(value_ref[:, 0:extent], probs, 1, 0).astype(BF16)
        log_ref[0, :, span] = log_total


def attend(qkv, starts, first, heads):
    every, tokens = qkv.shape[0] // (3 * HEAD_DIM), qkv.shape[1]

    def piece(offset):
        return pl.BlockSpec((HEAD_DIM, tokens), lambda h: (offset * every + first + h, 0))

    return pl.pallas_call(
        attend_kernel,
        grid=(heads,),
        in_specs=[piece(0), piece(1), piece(2), pl.BlockSpec((1, tokens), lambda h: (0, 0))],
        out_specs=[
            pl.BlockSpec((HEAD_DIM, tokens), lambda h: (h, 0)),
            pl.BlockSpec((1, 1, tokens), lambda h: (h, 0, 0)),
        ],
        out_shape=[
            jax.ShapeDtypeStruct((heads * HEAD_DIM, tokens), BF16),
            jax.ShapeDtypeStruct((heads, 1, tokens), F32),
        ],
        scratch_shapes=[pltpu.VMEM((tokens, HEAD_DIM), BF16)],
        name="attend",
    )(qkv, qkv, qkv, starts)


def attend_back_kernel(
    query_ref, key_ref, value_ref, start_ref, log_ref, grad_ref, out_ref,
    back_ref, sums_ref, keys, values, grad_keys, grad_values,
):
    scale = HEAD_DIM ** (-0.5)
    keys[...] = key_ref[...].T
    values[...] = value_ref[...].T
    tokens = query_ref.shape[1]
    grad_keys[...] = jnp.zeros_like(grad_keys)
    grad_values[...] = jnp.zeros_like(grad_values)
    query_sum = jnp.zeros((HEAD_DIM, 1), F32)
    for begin in range(0, tokens, QUERY_BLOCK):
        extent = begin + QUERY_BLOCK
        span = slice(begin, extent)
        query = query_ref[:, span]
        grad = grad_ref[:, span]
        grad_b = grad.astype(BF16)
        delta = jnp.sum(grad * out_ref[:, span].astype(F32), 0, keepdims=True)
        masked = scores_of(keys, query, start_ref[:, span], begin, extent)
        probs = jnp.exp(masked - log_ref[0, :, span])
        grad_probs = dot(values[0:extent, :], grad_b, 1, 0)
        grad_scores = (probs * (grad_probs - delta)).astype(BF16)
        grad_query = dot(key_ref[:, 0:extent], grad_scores, 1, 0) * scale
        query_sum += jnp.sum(grad_query, 1, keepdims=True)
        back_ref[0, :, span] = grad_query.astype(BF16)
        grad_keys[:, 0:extent] += dot(query, grad_scores, 1, 1)
        grad_values[:, 0:extent] += dot(grad_b, probs.astype(BF16), 1, 1)
    grad_value = grad_values[...]
    back_ref[1] = (grad_keys[...] * scale).astype(BF16)
    back_ref[2] = grad_value.astype(BF16)
    sums_ref[0] = jnp.broadcast_to(query_sum, sums_ref.shape[1:])
    sums_ref[1] = jnp.broadcast_to(
        jnp.sum(grad_value, 1, keepdims=True), sums_ref.shape[1:]
    )


def attend_back(qkv, starts, log_total, grad_attended, attended):
    heads, tokens = qkv.shape[0] // (3 * HEAD_DIM), qkv.shape[1]

    def piece(offset):
        return pl.BlockSpec((HEAD_DIM, tokens), lambda h: (offset * heads + h, 0))

    back, sums = pl.pallas_call(
        attend_back_kernel,
        grid=(heads,),
        in_specs=[
            piece(0), piece(1), piece(2),
            pl.BlockSpec((1, tokens), lambda h: (0, 0)),
            pl.BlockSpec((1, 1, tokens), lambda h: (h, 0, 0)),
            piece(0), piece(0),
        ],
        out_specs=[
            pl.BlockSpec((3, HEAD_DIM, tokens), lambda h: (0, h, 0)),
            pl.BlockSpec((2, HEAD_DIM, 128), lambda h: (0, h, 0)),
        ],
        out_shape=[
            jax.ShapeDtypeStruct((3, heads * HEAD_DIM, tokens), BF16),
            jax.ShapeDtypeStruct((2, heads * HEAD_DIM, 128), F32),
        ],
        scratch_shapes=[
            pltpu.VMEM((tokens, HEAD_DIM), BF16),
            pltpu.VMEM((tokens, HEAD_DIM), BF16),
            pltpu.VMEM((HEAD_DIM, tokens), F32),
            pltpu.VMEM((HEAD_DIM, tokens), F32),
        ],
        name="attend_back",
    )(qkv, qkv, qkv, starts, log_total, grad_attended, attended)
    return back.reshape(3 * heads * HEAD_DIM, tokens), sums[:, :, 0]


def norm_stats(inputs):
    mean = jnp.sum(inputs, 0) / D
    variance = jnp.sum(inputs * inputs, 0) / D - mean * mean
    return mean, lax.rsqrt(variance + EPSILON)


def center(inputs, stats):
    return (inputs - stats[0][None]) * stats[1][None]


def norm_back_sums(grad_normed, centered, gain):
    weighted = grad_normed * gain[:, None]
    return jnp.stack([jnp.sum(weighted, 0), jnp.sum(weighted * centered, 0)])


def norm_back(grad_normed, centered, inv_std, gain, sums):
    return inv_std[None] * (
        grad_normed * gain[:, None] - sums[0][None] / D - centered * (sums[1][None] / D)
    )


def per_device(
    tokens,
    cotangent,
    segment_ids,
    ln1_gain,
    ln1_shift,
    w_query,
    w_key,
    w_value,
    bias_query,
    bias_value,
    w_out,
    bias_out,
    ln2_gain,
    ln2_shift,
    w_up,
    bias_up,
    w_down,
    bias_down,
):
    narrow, wide = lax.axis_size("narrow"), lax.axis_size("wide")
    index = lax.axis_index("narrow")
    feats, toks = tokens.shape
    shard_rows = w_query.shape[0]
    own_cols = (HEADS - 1) // narrow * HEAD_DIM
    head_cols = own_cols + HEAD_DIM
    last = (HEADS - 1) * HEAD_DIM

    qkv_pieces = narrow_pieces(jnp.concatenate([w_query, w_key, w_value], 0))
    inputs = jnp.concatenate(narrow_pieces(tokens), 0)
    vectors = [ln1_gain, ln1_shift, bias_out, ln2_gain, ln2_shift, bias_query, bias_value]
    small = narrow_pieces(jnp.concatenate(vectors))

    def vector(k, pieces):
        return jnp.concatenate([piece[k * feats : (k + 1) * feats] for piece in pieces])

    gain1, shift1, bias_o, gain2, shift2 = [vector(k, small) for k in range(5)]
    small_ordered = in_order(small)
    bias_q, bias_v = vector(5, small_ordered), vector(6, small_ordered)
    qkv_rows = jnp.concatenate(in_order(qkv_pieces), 1)

    def heads_of(array):
        own = lax.dynamic_slice_in_dim(array, index * own_cols, own_cols, array.ndim - 1)
        return jnp.concatenate([own, array[..., last:]], -1)

    head_rows = heads_of(qkv_rows)
    attention_shard = jnp.concatenate(
        [head_rows[k * shard_rows : (k + 1) * shard_rows] for k in range(3)] + [w_out], 1
    )

    (up_cols,), _ = wide_gather(w_up, [(w_up.shape[1], feature_place)])
    (w_qkv, out_cols), hops = wide_gather(
        attention_shard, [(3 * head_cols, feature_place), (feats, lambda device: device)]
    )
    down_shard = jnp.concatenate(
        narrow_exchange(rows_to_blocks(after(w_down, hops[2]))), 1
    )
    down_block = lax.all_gather(down_shard, "wide", axis=0, tiled=True)
    cot_full = jnp.concatenate(narrow_pieces(after(cotangent, hops[1])), 0)
    out_pieces = narrow_pieces(out_cols)
    out_full = jnp.concatenate(out_pieces, 1)

    rows_f = inputs.astype(F32)
    stats1 = norm_stats(rows_f)
    centered1 = center(rows_f, stats1)
    normed1 = (centered1 * gain1[:, None] + shift1[:, None]).astype(BF16)
    bias_qkv = jnp.concatenate(
        [heads_of(bias_q), jnp.zeros((head_cols,), F32), heads_of(bias_v)]
    )
    qkv = (dot(after(w_qkv, down_shard), normed1, 0, 0) + bias_qkv[:, None]).astype(BF16)
    starts = jnp.sum(
        (segment_ids[:, None] < segment_ids[None, :]).astype(jnp.int32), 0, keepdims=True
    )
    some = own_cols // HEAD_DIM // 2
    attended1, log1 = attend(qkv, starts, 0, some)
    held = after(qkv, attended1, out_pieces[1])
    attended2, log2 = attend(held, starts, some, some)
    attended_own = jnp.concatenate([attended1, attended2], 0)
    attended_pieces = narrow_pieces(attended_own)
    attended3, log3 = attend(held, starts, 2 * some, 1)
    attended = jnp.concatenate([attended_own, attended3], 0)
    log_total = jnp.concatenate([log1, log2, log3], 0)
    attended_full = jnp.concatenate(in_order(attended_pieces) + [attended3], 0)
    resid = rows_f + dot(out_full, attended_full, 0, 0) + bias_o[:, None]

    stats2 = norm_stats(resid)
    centered2 = center(resid, stats2)
    normed2 = (centered2 * gain2[:, None] + shift2[:, None]).astype(BF16)
    hidden_pre = dot(up_cols, normed2, 0, 0) + bias_up[:, None]
    hidden, gelu_back = jax.vjp(gelu_tanh, hidden_pre)
    hidden = hidden.astype(BF16)
    grad_hidden = dot(down_block, cot_full, 1, 0)
    grad_pre = gelu_back(grad_hidden)[0]
    grad_pre_b = grad_pre.astype(BF16)
    grad_normed2 = dot(up_cols, grad_pre_b, 1, 0)
    sums2 = narrow_total(norm_back_sums(grad_normed2, centered2, gain2))
    grad_normed2_own = narrow_scatter(grad_normed2)

    resid_own = resid[:feats]
    output = (
        resid_own + (narrow_scatter(dot(down_block, hidden, 0, 0)) + bias_down[:, None])
    ).astype(BF16)
    grad_up = dot(normed2, grad_pre_b, 1, 1).astype(BF16)
    grad_down = dot(hidden, cot_full, 1, 1).astype(BF16)
    grad_up = jnp.concatenate(
        in_order([grad_up[k * feats : (k + 1) * feats] for k in range(narrow)]), 0
    )
    sum_down = lax.psum_scatter(grad_down, "wide", scatter_dimension=0, tiled=True)
    grad_up = after(grad_up, grad_down)
    sum_up = lax.psum_scatter(grad_up, "wide", scatter_dimension=0, tiled=True)
    cot_own = cotangent.astype(F32)
    centered2_own = center(resid_own, stats2)
    grad_resid = cot_own + norm_back(
        grad_normed2_own, centered2_own, stats2[1], ln2_gain, sums2
    )
    grad_resid_own = grad_resid.astype(BF16)
    grad_resid_b = jnp.concatenate(narrow_pieces(grad_resid_own), 0)

    out_heads = jnp.concatenate(
        [lax.dynamic_slice_in_dim(out_full, index * own_cols, own_cols, 0), out_full[last:]], 0
    )
    grad_attended = dot(out_heads, grad_resid_b, 1, 0)
    grad_qkv, head_sums = attend_back(qkv, starts, log_total, grad_attended, attended)
    grad_wout = dot(attended_full, after(grad_resid_own, grad_up), 1, 1).astype(BF16)
    keep_last = (index == narrow - 1).astype(BF16)
    row_ids = jnp.arange(3 * head_cols) % head_cols
    counted = jnp.where(row_ids < own_cols, jnp.ones((), BF16), keep_last)
    grad_normed1 = dot(w_qkv, grad_qkv * counted[:, None], 1, 0)
    sums1 = narrow_total(norm_back_sums(grad_normed1, centered1, gain1))
    stages = narrow_stages(grad_normed1)
    grad_normed1_own = stages[-1]
    half = (3 * head_cols + feats) // 256 * 128 + 128
    grads = [
        dot(normed1, grad, 1, 1).astype(BF16).reshape(wide, shard_rows, -1)
        for grad in (grad_qkv[:half], grad_qkv[half:])
    ]
    grad_wout = grad_wout.reshape(wide, shard_rows, -1)
    waits = {2: stages[1], 6: stages[-1]}
    sum_first = wide_scatter([(grads[0], feature_place)], 1, waits)
    sum_rest = wide_scatter(
        [(grads[1], feature_place), (grad_wout, lambda device: device)], -1, waits
    )
    sum_qkv = jnp.concatenate([sum_first, sum_rest[:, :-feats]], -1)
    sum_wo = sum_rest[:, -feats:]
    sum_down = after(sum_down, stages[-1])
    sum_down = blocks_to_rows(
        narrow_exchange([sum_down[:, k * feats : (k + 1) * feats] for k in range(narrow)])
    )
    sum_heads = jnp.concatenate(
        [sum_qkv[:, k * head_cols : (k + 1) * head_cols] for k in range(3)], 0
    )
    sum_cols = jnp.concatenate(
        in_order(narrow_pieces(sum_heads[:, :own_cols])) + [sum_heads[:, own_cols:]], 1
    )
    sum_own = lax.select_n(
        index, *[sum_cols[:, k * feats : (k + 1) * feats] for k in range(narrow)]
    ).astype(F32)

    centered1_own = center(tokens.astype(F32), stats1)
    grad_tokens = grad_resid + norm_back(
        grad_normed1_own, centered1_own, stats1[1], ln1_gain, sums1
    )

    placed = lax.dynamic_update_slice_in_dim(
        jnp.zeros((2, D), F32), head_sums[:, :own_cols], index * own_cols, 1
    )
    tail = jnp.where(index == narrow - 1, head_sums[:, own_cols:], 0.0)
    placed = lax.dynamic_update_slice_in_dim(placed, tail, last, 1)
    head_total = lax.dynamic_slice_in_dim(narrow_total(placed), index * feats, feats, 1)
    pieces = [
        jnp.sum(grad_normed1_own * centered1_own, 1),
        jnp.sum(grad_normed1_own, 1),
        head_total[0],
        head_total[1],
        jnp.sum(grad_resid, 1),
        jnp.sum(grad_normed2_own * centered2_own, 1),
        jnp.sum(grad_normed2_own, 1),
        jnp.sum(cot_own, 1),
        jnp.sum(grad_pre, 1),
    ]
    total = wide_total(jnp.concatenate(pieces))
    sums = [total[k * feats : (k + 1) * feats] for k in range(8)]
    return (
        output,
        grad_tokens,
        sums[0],
        sums[1],
        sum_own[:shard_rows],
        sum_own[shard_rows : 2 * shard_rows],
        sum_own[2 * shard_rows :],
        sums[2],
        sums[3],
        sum_wo.astype(F32),
        sums[4],
        sums[5],
        sums[6],
        sum_up.astype(F32),
        total[8 * feats :],
        sum_down.astype(F32),
        sums[7],
    )


def solution(mesh):
    matrix, vector = P("wide", "narrow"), P("narrow")
    acts = P("narrow", "wide")
    return jax.shard_map(
        per_device,
        mesh=mesh,
        in_specs=(
            acts, acts, P("wide"), vector, vector, matrix, matrix, matrix, vector, vector,
            matrix, vector, vector, vector, matrix, vector, matrix, vector,
        ),
        out_specs=(
            acts, acts, vector, vector, matrix, matrix, matrix, vector, vector,
            matrix, vector, vector, vector, matrix, vector, matrix, vector,
        ),
        check_vma=False,
    )
```

```python
import functools

import jax
import jax.numpy as jnp
from jax import lax
from jax.experimental import pallas as pl
from jax.experimental.pallas import tpu as pltpu
from jax.sharding import PartitionSpec as P

D = 1088
HEADS = 17
HEAD_DIM = 64
SEQ_LEN = 1024
QUERY_BLOCK = 256
EPSILON = 1e-05
MASKED = -1e30
F32 = jnp.float32
BF16 = jnp.bfloat16


def dot(left_side, right_side, left_dim, right_dim):
    return lax.dot_general(
        left_side,
        right_side,
        (((left_dim,), (right_dim,)), ((), ())),
        preferred_element_type=F32,
    )


def gelu_tanh(values):
    return jax.nn.gelu(values, approximate=True)


def narrow_bits():
    count = lax.axis_size("narrow")
    return [1 << b for b in range(count.bit_length() - 1)]


def reverse_bits(value):
    bits = narrow_bits()
    last = len(bits) - 1
    return sum(((value >> k) & 1) << (last - k) for k in range(len(bits)))


def swap_narrow(value, mask):
    count = lax.axis_size("narrow")
    return lax.ppermute(value, "narrow", [(a, a ^ mask) for a in range(count)])


def narrow_pieces(block):
    held = {0: block}
    for bit in reversed(narrow_bits()):
        held.update({m ^ bit: swap_narrow(v, bit) for m, v in list(held.items())})
    return [held[reverse_bits(p)] for p in range(len(held))]


def in_order(pieces):
    index = lax.axis_index("narrow")
    by_mask = [pieces[reverse_bits(m)] for m in range(len(pieces))]
    return [lax.select_n(index ^ k, *by_mask) for k in range(len(pieces))]


def narrow_scatter(partial):
    return narrow_stages(partial)[-1]


def narrow_stages(partial):
    stages = [partial]
    for bit in narrow_bits():
        half = stages[-1].shape[0] // 2
        came = swap_narrow(stages[-1][half:].astype(BF16), bit)
        stages.append(stages[-1][:half] + came.astype(F32))
    return stages


def narrow_total(value):
    for bit in narrow_bits():
        value = value + swap_narrow(value, bit)
    return value


def narrow_exchange(blocks):
    return [
        swap_narrow(block, reverse_bits(p)) if p else block for p, block in enumerate(blocks)
    ]


def ring_place(device, count):
    return (device >> 1) ^ ((device & 1) * (count - 1))


def ring_device(place, count):
    return jnp.where(place < count // 2, 2 * place, 2 * (count - 1 - place) + 1)


def ring_step(value, direction):
    count = lax.axis_size("wide")
    order = list(range(0, count, 2)) + list(range(count - 1, 0, -2))
    return lax.ppermute(
        value, "wide", [(order[k], order[(k + direction) % count]) for k in range(count)]
    )


def feature_place(device):
    each = lax.axis_size("wide") // lax.axis_size("narrow")
    block = device >> (each.bit_length() - 1)
    return reverse_bits(block ^ lax.axis_index("narrow")) * each + (device & (each - 1))


def place_kernel(where_ref, *refs, count):
    pieces, outs = refs[:count], refs[count:]
    for k, piece in enumerate(pieces):
        begin = 0
        for part, out_ref in enumerate(outs):
            cols = out_ref.shape[2]
            out_ref[where_ref[part, k]] = piece[:, begin : begin + cols]
            begin += cols


def wide_gather(block, parts, waits):
    count = lax.axis_size("wide")
    cut = block.shape[0] // 16 * 8
    pieces, hops = [block], [0]
    ahead = behind = block
    for hop in range(1, count // 2):
        if hop in waits:
            ahead, behind = after(ahead, *waits[hop]), after(behind, *waits[hop])
        ahead, behind = lax.optimization_barrier((ring_step(ahead, 1), ring_step(behind, -1)))
        pieces += [ahead, behind]
        hops += [-hop, hop]
    far = jnp.concatenate([ring_step(ahead[:cut], 1), ring_step(behind[cut:], -1)], 0)
    pieces.append(far)
    hops.append(count // 2)
    here = ring_place(lax.axis_index("wide"), count)
    devices = ring_device((here + jnp.array(hops)) & (count - 1), count)
    places = jnp.stack([place_of(devices) for _, place_of in parts]).astype(jnp.int32)
    rows = block.shape[0]
    wholes = pl.pallas_call(
        functools.partial(place_kernel, count=count),
        grid_spec=pltpu.PrefetchScalarGridSpec(
            num_scalar_prefetch=1,
            grid=(1,),
            in_specs=[pl.BlockSpec(block.shape, lambda i, w: (0, 0))] * count,
            out_specs=[
                pl.BlockSpec((count, rows, width), lambda i, w: (0, 0, 0)) for width, _ in parts
            ],
        ),
        out_shape=[
            jax.ShapeDtypeStruct((count, rows, width), block.dtype) for width, _ in parts
        ],
        name="place_blocks",
    )(places, *pieces)
    return [whole.reshape(count * rows, whole.shape[2]) for whole in wholes], pieces


def wide_scatter(groups, waits):
    count = lax.axis_size("wide")
    here = ring_place(lax.axis_index("wide"), count)
    directions = (1, -1)

    def part(partials, direction, back):
        device = ring_device((here - direction * back) & (count - 1), count)
        return jnp.concatenate(
            [
                lax.dynamic_index_in_dim(partial, place_of(device), 0, keepdims=False)
                for partial, place_of in partials
            ],
            -1,
        )

    moving = [part(g, d, 1).astype(BF16) for g, d in zip(groups, directions)]
    for hop in range(1, count):
        if hop in waits:
            moving = [after(m, *waits[hop]) for m in moving]
        came = lax.optimization_barrier(
            tuple(ring_step(m, d) for m, d in zip(moving, directions))
        )
        moving = [
            (c.astype(F32) + part(g, d, hop + 1).astype(F32)).astype(BF16)
            for c, g, d in zip(came, groups, directions)
        ]
    return moving


def wide_total(value):
    count = lax.axis_size("wide")
    bit = 1
    while bit < count:
        value = value + lax.ppermute(value, "wide", [(a, a ^ bit) for a in range(count)])
        bit *= 2
    return value


def turn_pairs(turn):
    wide, narrow = lax.axis_size("wide"), lax.axis_size("narrow")
    each = wide // narrow
    return [
        (each * b + h, narrow * h + (b + turn) % narrow)
        for b in range(narrow)
        for h in range(each)
    ]


def rows_to_blocks(shard, hops):
    wide, narrow = lax.axis_size("wide"), lax.axis_size("narrow")
    device, index = lax.axis_index("wide"), lax.axis_index("narrow")
    block = device >> ((wide // narrow).bit_length() - 1)
    rows = shard.shape[0] // narrow
    came = []
    for turn in range(narrow):
        start = ((block + turn) & (narrow - 1)) * rows
        leaving = lax.dynamic_slice_in_dim(shard, start, rows, 0)
        leaving = after(leaving, hops[1 if turn < narrow // 2 else 3])
        came.append(lax.ppermute(leaving, "wide", turn_pairs(turn)))
    came = [after(part, hops[-1]) for part in came]
    return [
        lax.select_n((device - (index ^ reverse_bits(p))) & (narrow - 1), *came)
        for p in range(narrow)
    ]


def blocks_to_rows(parts):
    wide, narrow = lax.axis_size("wide"), lax.axis_size("narrow")
    device, index = lax.axis_index("wide"), lax.axis_index("narrow")
    block = device >> ((wide // narrow).bit_length() - 1)
    came = []
    for turn in range(narrow):
        pairs = [(b, a) for a, b in turn_pairs(turn)]
        leaving = lax.select_n(
            reverse_bits(((device - turn) & (narrow - 1)) ^ index), *parts
        )
        came.append(lax.ppermute(leaving, "wide", pairs))
    return jnp.concatenate(
        [lax.select_n((k - block) & (narrow - 1), *came) for k in range(narrow)], 0
    )


def after(value, *others):
    return lax.optimization_barrier((value, *others))[0]


def scores_of(keys, query, starts, begin, extent):
    scores = dot(keys[0:extent, :], query * HEAD_DIM ** (-0.5), 1, 0)
    key_pos = lax.broadcasted_iota(jnp.int32, scores.shape, 0)
    query_pos = begin + lax.broadcasted_iota(jnp.int32, scores.shape, 1)
    return jnp.where((key_pos >= starts) & (key_pos <= query_pos), scores, MASKED)


def attend_kernel(query_ref, key_ref, value_ref, start_ref, out_ref, log_ref, keys):
    keys[...] = key_ref[...].T
    tokens = query_ref.shape[1]
    for begin in range(0, tokens, QUERY_BLOCK):
        extent = begin + QUERY_BLOCK
        span = slice(begin, extent)
        masked = scores_of(keys, query_ref[:, span], start_ref[:, span], begin, extent)
        top = jnp.max(masked, 0, keepdims=True)
        powers = jnp.exp(masked - top)
        total = jnp.sum(powers, 0, keepdims=True)
        log_total = top + jnp.log(total)
        probs = (powers * (1.0 / total)).astype(BF16)
        out_ref[:, span] = dot(value_ref[:, 0:extent], probs, 1, 0).astype(BF16)
        log_ref[0, :, span] = log_total


def attend(qkv, starts, first, heads):
    every, tokens = qkv.shape[0] // (3 * HEAD_DIM), qkv.shape[1]

    def piece(offset):
        return pl.BlockSpec((HEAD_DIM, tokens), lambda h: (offset * every + first + h, 0))

    return pl.pallas_call(
        attend_kernel,
        grid=(heads,),
        in_specs=[piece(0), piece(1), piece(2), pl.BlockSpec((1, tokens), lambda h: (0, 0))],
        out_specs=[
            pl.BlockSpec((HEAD_DIM, tokens), lambda h: (h, 0)),
            pl.BlockSpec((1, 1, tokens), lambda h: (h, 0, 0)),
        ],
        out_shape=[
            jax.ShapeDtypeStruct((heads * HEAD_DIM, tokens), BF16),
            jax.ShapeDtypeStruct((heads, 1, tokens), F32),
        ],
        scratch_shapes=[pltpu.VMEM((tokens, HEAD_DIM), BF16)],
        name="attend",
    )(qkv, qkv, qkv, starts)


def attend_back_kernel(
    query_ref, key_ref, value_ref, start_ref, log_ref, grad_ref, out_ref,
    back_ref, sums_ref, keys, values, grad_keys, grad_values,
):
    scale = HEAD_DIM ** (-0.5)
    keys[...] = key_ref[...].T
    values[...] = value_ref[...].T
    tokens = query_ref.shape[1]
    grad_keys[...] = jnp.zeros_like(grad_keys)
    grad_values[...] = jnp.zeros_like(grad_values)
    query_sum = jnp.zeros((HEAD_DIM, 1), F32)
    for begin in range(0, tokens, QUERY_BLOCK):
        extent = begin + QUERY_BLOCK
        span = slice(begin, extent)
        query = query_ref[:, span]
        grad = grad_ref[:, span]
        grad_b = grad.astype(BF16)
        delta = jnp.sum(grad * out_ref[:, span].astype(F32), 0, keepdims=True)
        masked = scores_of(keys, query, start_ref[:, span], begin, extent)
        probs = jnp.exp(masked - log_ref[0, :, span])
        grad_probs = dot(values[0:extent, :], grad_b, 1, 0)
        grad_scores = (probs * (grad_probs - delta)).astype(BF16)
        grad_query = dot(key_ref[:, 0:extent], grad_scores, 1, 0) * scale
        query_sum += jnp.sum(grad_query, 1, keepdims=True)
        back_ref[0, :, span] = grad_query.astype(BF16)
        grad_keys[:, 0:extent] += dot(query, grad_scores, 1, 1)
        grad_values[:, 0:extent] += dot(grad_b, probs.astype(BF16), 1, 1)
    grad_value = grad_values[...]
    back_ref[1] = (grad_keys[...] * scale).astype(BF16)
    back_ref[2] = grad_value.astype(BF16)
    sums_ref[0] = jnp.broadcast_to(query_sum, sums_ref.shape[1:])
    sums_ref[1] = jnp.broadcast_to(
        jnp.sum(grad_value, 1, keepdims=True), sums_ref.shape[1:]
    )


def attend_back(qkv, starts, log_total, grad_attended, attended):
    heads, tokens = qkv.shape[0] // (3 * HEAD_DIM), qkv.shape[1]

    def piece(offset):
        return pl.BlockSpec((HEAD_DIM, tokens), lambda h: (offset * heads + h, 0))

    back, sums = pl.pallas_call(
        attend_back_kernel,
        grid=(heads,),
        in_specs=[
            piece(0), piece(1), piece(2),
            pl.BlockSpec((1, tokens), lambda h: (0, 0)),
            pl.BlockSpec((1, 1, tokens), lambda h: (h, 0, 0)),
            piece(0), piece(0),
        ],
        out_specs=[
            pl.BlockSpec((3, HEAD_DIM, tokens), lambda h: (0, h, 0)),
            pl.BlockSpec((2, HEAD_DIM, 128), lambda h: (0, h, 0)),
        ],
        out_shape=[
            jax.ShapeDtypeStruct((3, heads * HEAD_DIM, tokens), BF16),
            jax.ShapeDtypeStruct((2, heads * HEAD_DIM, 128), F32),
        ],
        scratch_shapes=[
            pltpu.VMEM((tokens, HEAD_DIM), BF16),
            pltpu.VMEM((tokens, HEAD_DIM), BF16),
            pltpu.VMEM((HEAD_DIM, tokens), F32),
            pltpu.VMEM((HEAD_DIM, tokens), F32),
        ],
        name="attend_back",
    )(qkv, qkv, qkv, starts, log_total, grad_attended, attended)
    return back.reshape(3 * heads * HEAD_DIM, tokens), sums[:, :, 0]


def norm_stats(inputs):
    mean = jnp.sum(inputs, 0) / D
    variance = jnp.sum(inputs * inputs, 0) / D - mean * mean
    return mean, lax.rsqrt(variance + EPSILON)


def center(inputs, stats):
    return (inputs - stats[0][None]) * stats[1][None]


def norm_back_sums(grad_normed, centered, gain):
    weighted = grad_normed * gain[:, None]
    return jnp.stack([jnp.sum(weighted, 0), jnp.sum(weighted * centered, 0)])


def norm_back(grad_normed, centered, inv_std, gain, sums):
    return inv_std[None] * (
        grad_normed * gain[:, None] - sums[0][None] / D - centered * (sums[1][None] / D)
    )


def per_device(
    tokens,
    cotangent,
    segment_ids,
    ln1_gain,
    ln1_shift,
    w_query,
    w_key,
    w_value,
    bias_query,
    bias_value,
    w_out,
    bias_out,
    ln2_gain,
    ln2_shift,
    w_up,
    bias_up,
    w_down,
    bias_down,
):
    narrow, wide = lax.axis_size("narrow"), lax.axis_size("wide")
    index = lax.axis_index("narrow")
    feats, toks = tokens.shape
    shard_rows = w_query.shape[0]
    own_cols = (HEADS - 1) // narrow * HEAD_DIM
    head_cols = own_cols + HEAD_DIM
    last = (HEADS - 1) * HEAD_DIM

    qkv_pieces = narrow_pieces(jnp.concatenate([w_query, w_key, w_value], 0))
    token_pieces = narrow_pieces(tokens)
    inputs = jnp.concatenate(token_pieces, 0)
    vectors = [ln1_gain, ln1_shift, bias_out, ln2_gain, ln2_shift, bias_query, bias_value]
    small = narrow_pieces(jnp.concatenate(vectors))

    def vector(k, pieces):
        return jnp.concatenate([piece[k * feats : (k + 1) * feats] for piece in pieces])

    gain1, shift1, bias_o, gain2, shift2 = [vector(k, small) for k in range(5)]
    small_ordered = in_order(small)
    bias_q, bias_v = vector(5, small_ordered), vector(6, small_ordered)
    qkv_rows = jnp.concatenate(in_order(qkv_pieces), 1)

    def heads_of(array):
        own = lax.dynamic_slice_in_dim(array, index * own_cols, own_cols, array.ndim - 1)
        return jnp.concatenate([own, array[..., last:]], -1)

    head_rows = heads_of(qkv_rows)
    attention_shard = jnp.concatenate(
        [head_rows[k * shard_rows : (k + 1) * shard_rows] for k in range(3)] + [w_out], 1
    )

    (w_qkv, out_cols), hops = wide_gather(
        attention_shard,
        [(3 * head_cols, feature_place), (feats, lambda device: device)],
        {2: token_pieces[1:2], 3: (*token_pieces, *small)},
    )
    (up_cols,), up_hops = wide_gather(after(w_up, hops[5]), [(w_up.shape[1], feature_place)], {})
    down_shard = jnp.concatenate(
        narrow_exchange(rows_to_blocks(w_down, hops)), 1
    )
    down_block = lax.all_gather(down_shard, "wide", axis=0, tiled=True)
    cot_full = jnp.concatenate(narrow_pieces(after(cotangent, hops[1])), 0)
    out_pieces = narrow_pieces(out_cols)
    out_full = jnp.concatenate(out_pieces, 1)

    rows_f = inputs.astype(F32)
    stats1 = norm_stats(rows_f)
    centered1 = center(rows_f, stats1)
    normed1 = (centered1 * gain1[:, None] + shift1[:, None]).astype(BF16)
    bias_qkv = jnp.concatenate(
        [heads_of(bias_q), jnp.zeros((head_cols,), F32), heads_of(bias_v)]
    )
    qkv = (dot(w_qkv, normed1, 0, 0) + bias_qkv[:, None]).astype(BF16)
    starts = jnp.sum(
        (segment_ids[:, None] < segment_ids[None, :]).astype(jnp.int32), 0, keepdims=True
    )
    some = own_cols // HEAD_DIM // 2
    held = after(qkv, *up_hops[1:3])
    attended1, log1 = attend(held, starts, 0, some)
    held = after(held, attended1, out_pieces[1], down_shard, *up_hops[3:5])
    attended2, log2 = attend(held, starts, some, some)
    attended_own = jnp.concatenate([attended1, attended2], 0)
    attended_pieces = narrow_pieces(attended_own)
    attended3, log3 = attend(held, starts, 2 * some, 1)
    attended = jnp.concatenate([attended_own, attended3], 0)
    log_total = jnp.concatenate([log1, log2, log3], 0)
    attended_full = jnp.concatenate(in_order(attended_pieces) + [attended3], 0)
    resid = rows_f + dot(out_full, attended_full, 0, 0) + bias_o[:, None]

    stats2 = norm_stats(resid)
    centered2 = center(resid, stats2)
    normed2 = (centered2 * gain2[:, None] + shift2[:, None]).astype(BF16)
    hidden_pre = dot(up_cols, normed2, 0, 0) + bias_up[:, None]
    hidden, gelu_back = jax.vjp(gelu_tanh, hidden_pre)
    hidden = hidden.astype(BF16)
    grad_hidden = dot(down_block, cot_full, 1, 0)
    grad_pre = gelu_back(grad_hidden)[0]
    grad_pre_b = grad_pre.astype(BF16)
    grad_normed2 = dot(up_cols, grad_pre_b, 1, 0)
    sums2 = narrow_total(norm_back_sums(grad_normed2, centered2, gain2))
    grad_normed2_own = narrow_scatter(grad_normed2)

    resid_own = resid[:feats]
    grad_up = dot(normed2, grad_pre_b, 1, 1).astype(BF16)
    grad_down = dot(hidden, cot_full, 1, 1).astype(BF16)
    grad_up = jnp.concatenate(
        in_order([grad_up[k * feats : (k + 1) * feats] for k in range(narrow)]), 0
    )
    sum_down = lax.psum_scatter(grad_down, "wide", scatter_dimension=0, tiled=True)
    grad_up = after(grad_up, grad_down)
    sum_up = lax.psum_scatter(grad_up, "wide", scatter_dimension=0, tiled=True)
    cot_own = cotangent.astype(F32)
    centered2_own = center(resid_own, stats2)
    grad_resid = cot_own + norm_back(
        grad_normed2_own, centered2_own, stats2[1], ln2_gain, sums2
    )
    grad_resid_own = grad_resid.astype(BF16)
    grad_resid_b = jnp.concatenate(narrow_pieces(grad_resid_own), 0)
    output_part = dot(down_block, after(hidden, grad_resid_own), 0, 0)
    output = (resid_own + (narrow_scatter(output_part) + bias_down[:, None])).astype(BF16)

    out_heads = jnp.concatenate(
        [lax.dynamic_slice_in_dim(out_full, index * own_cols, own_cols, 0), out_full[last:]], 0
    )
    grad_attended = dot(out_heads, grad_resid_b, 1, 0)
    sum_down = after(sum_down, grad_attended)
    down_parts = narrow_exchange(
        [sum_down[:, k * feats : (k + 1) * feats] for k in range(narrow)]
    )
    grad_qkv, head_sums = attend_back(qkv, starts, log_total, grad_attended, attended)
    grad_wout = dot(attended_full, after(grad_resid_own, grad_up), 1, 1).astype(BF16)
    keep_last = (index == narrow - 1).astype(BF16)
    row_ids = jnp.arange(3 * head_cols) % head_cols
    counted = jnp.where(row_ids < own_cols, jnp.ones((), BF16), keep_last)
    grad_normed1 = dot(w_qkv, grad_qkv * counted[:, None], 1, 0)
    sums1 = narrow_total(norm_back_sums(grad_normed1, centered1, gain1))
    stages = narrow_stages(grad_normed1)
    grad_normed1_own = stages[-1]
    half = (3 * head_cols + feats) // 256 * 128 + 128
    grads = [
        dot(normed1, grad, 1, 1).astype(BF16).reshape(wide, shard_rows, -1)
        for grad in (grad_qkv[:half], grad_qkv[half:])
    ]
    grad_wout = grad_wout.reshape(wide, shard_rows, -1)
    waits = {2: stages[1], 6: stages[-1]}
    sum_down = blocks_to_rows(down_parts)
    sum_first, sum_rest = wide_scatter(
        [
            [(grads[0], feature_place)],
            [(grads[1], feature_place), (grad_wout, lambda device: device)],
        ],
        {2: (stages[1],), 4: down_parts[1:], 6: (stages[-1], sum_down)},
    )
    sum_qkv = jnp.concatenate([sum_first, sum_rest[:, :-feats]], -1)
    sum_wo = sum_rest[:, -feats:]
    sum_heads = jnp.concatenate(
        [sum_qkv[:, k * head_cols : (k + 1) * head_cols] for k in range(3)], 0
    )
    sum_cols = jnp.concatenate(
        in_order(narrow_pieces(sum_heads[:, :own_cols])) + [sum_heads[:, own_cols:]], 1
    )
    sum_own = lax.select_n(
        index, *[sum_cols[:, k * feats : (k + 1) * feats] for k in range(narrow)]
    ).astype(F32)

    centered1_own = center(tokens.astype(F32), stats1)
    grad_tokens = grad_resid + norm_back(
        grad_normed1_own, centered1_own, stats1[1], ln1_gain, sums1
    )

    placed = lax.dynamic_update_slice_in_dim(
        jnp.zeros((2, D), F32), head_sums[:, :own_cols], index * own_cols, 1
    )
    tail = jnp.where(index == narrow - 1, head_sums[:, own_cols:], 0.0)
    placed = lax.dynamic_update_slice_in_dim(placed, tail, last, 1)
    head_total = lax.dynamic_slice_in_dim(narrow_total(placed), index * feats, feats, 1)
    pieces = [
        jnp.sum(grad_normed1_own * centered1_own, 1),
        jnp.sum(grad_normed1_own, 1),
        head_total[0],
        head_total[1],
        jnp.sum(grad_resid, 1),
        jnp.sum(grad_normed2_own * centered2_own, 1),
        jnp.sum(grad_normed2_own, 1),
        jnp.sum(cot_own, 1),
        jnp.sum(grad_pre, 1),
    ]
    total = wide_total(jnp.concatenate(pieces))
    sums = [total[k * feats : (k + 1) * feats] for k in range(8)]
    return (
        output,
        grad_tokens,
        sums[0],
        sums[1],
        sum_own[:shard_rows],
        sum_own[shard_rows : 2 * shard_rows],
        sum_own[2 * shard_rows :],
        sums[2],
        sums[3],
        sum_wo.astype(F32),
        sums[4],
        sums[5],
        sums[6],
        sum_up.astype(F32),
        total[8 * feats :],
        sum_down.astype(F32),
        sums[7],
    )


def solution(mesh):
    matrix, vector = P("wide", "narrow"), P("narrow")
    acts = P("narrow", "wide")
    return jax.shard_map(
        per_device,
        mesh=mesh,
        in_specs=(
            acts, acts, P("wide"), vector, vector, matrix, matrix, matrix, vector, vector,
            matrix, vector, vector, vector, matrix, vector, matrix, vector,
        ),
        out_specs=(
            acts, acts, vector, vector, matrix, matrix, matrix, vector, vector,
            matrix, vector, vector, vector, matrix, vector, matrix, vector,
        ),
        check_vma=False,
    )
```

```python
import functools

import jax
import jax.numpy as jnp
from jax import lax
from jax.experimental import pallas as pl
from jax.experimental.pallas import tpu as pltpu
from jax.sharding import PartitionSpec as P

D = 1088
HEADS = 17
HEAD_DIM = 64
SEQ_LEN = 1024
QUERY_BLOCK = 256
EPSILON = 1e-05
MASKED = -1e30
F32 = jnp.float32
BF16 = jnp.bfloat16


def dot(left_side, right_side, left_dim, right_dim):
    return lax.dot_general(
        left_side,
        right_side,
        (((left_dim,), (right_dim,)), ((), ())),
        preferred_element_type=F32,
    )


def gelu_tanh(values):
    return jax.nn.gelu(values, approximate=True)


def narrow_bits():
    count = lax.axis_size("narrow")
    return [1 << b for b in range(count.bit_length() - 1)]


def reverse_bits(value):
    bits = narrow_bits()
    last = len(bits) - 1
    return sum(((value >> k) & 1) << (last - k) for k in range(len(bits)))


def swap_narrow(value, mask):
    count = lax.axis_size("narrow")
    return lax.ppermute(value, "narrow", [(a, a ^ mask) for a in range(count)])


def narrow_pieces(block):
    held = {0: block}
    for bit in reversed(narrow_bits()):
        held.update({m ^ bit: swap_narrow(v, bit) for m, v in list(held.items())})
    return [held[reverse_bits(p)] for p in range(len(held))]


def in_order(pieces):
    index = lax.axis_index("narrow")
    by_mask = [pieces[reverse_bits(m)] for m in range(len(pieces))]
    return [lax.select_n(index ^ k, *by_mask) for k in range(len(pieces))]


def narrow_scatter(partial):
    return narrow_stages(partial)[-1]


def narrow_stages(partial):
    stages = [partial]
    for bit in narrow_bits():
        half = stages[-1].shape[0] // 2
        came = swap_narrow(stages[-1][half:].astype(BF16), bit)
        stages.append(stages[-1][:half] + came.astype(F32))
    return stages


def narrow_total(value):
    for bit in narrow_bits():
        value = value + swap_narrow(value, bit)
    return value


def narrow_exchange(blocks):
    return [
        swap_narrow(block, reverse_bits(p)) if p else block for p, block in enumerate(blocks)
    ]


def ring_place(device, count):
    return (device >> 1) ^ ((device & 1) * (count - 1))


def ring_device(place, count):
    return jnp.where(place < count // 2, 2 * place, 2 * (count - 1 - place) + 1)


def ring_step(value, direction):
    count = lax.axis_size("wide")
    order = list(range(0, count, 2)) + list(range(count - 1, 0, -2))
    return lax.ppermute(
        value, "wide", [(order[k], order[(k + direction) % count]) for k in range(count)]
    )


def feature_place(device):
    each = lax.axis_size("wide") // lax.axis_size("narrow")
    block = device >> (each.bit_length() - 1)
    return reverse_bits(block ^ lax.axis_index("narrow")) * each + (device & (each - 1))


def place_kernel(where_ref, *refs, count):
    pieces, outs = refs[:count], refs[count:]
    for k, piece in enumerate(pieces):
        begin = 0
        for part, out_ref in enumerate(outs):
            cols = out_ref.shape[2]
            out_ref[where_ref[part, k]] = piece[:, begin : begin + cols]
            begin += cols


def wide_gather(block, parts, waits):
    count = lax.axis_size("wide")
    cut = block.shape[0] // 16 * 8
    pieces, hops = [block], [0]
    ahead = behind = block
    for hop in range(1, count // 2):
        if hop in waits:
            ahead, behind = after(ahead, *waits[hop]), after(behind, *waits[hop])
        ahead, behind = lax.optimization_barrier((ring_step(ahead, 1), ring_step(behind, -1)))
        pieces += [ahead, behind]
        hops += [-hop, hop]
    far = jnp.concatenate([ring_step(ahead[:cut], 1), ring_step(behind[cut:], -1)], 0)
    pieces.append(far)
    hops.append(count // 2)
    here = ring_place(lax.axis_index("wide"), count)
    devices = ring_device((here + jnp.array(hops)) & (count - 1), count)
    places = jnp.stack([place_of(devices) for _, place_of in parts]).astype(jnp.int32)
    rows = block.shape[0]
    wholes = pl.pallas_call(
        functools.partial(place_kernel, count=count),
        grid_spec=pltpu.PrefetchScalarGridSpec(
            num_scalar_prefetch=1,
            grid=(1,),
            in_specs=[pl.BlockSpec(block.shape, lambda i, w: (0, 0))] * count,
            out_specs=[
                pl.BlockSpec((count, rows, width), lambda i, w: (0, 0, 0)) for width, _ in parts
            ],
        ),
        out_shape=[
            jax.ShapeDtypeStruct((count, rows, width), block.dtype) for width, _ in parts
        ],
        name="place_blocks",
    )(places, *pieces)
    return [whole.reshape(count * rows, whole.shape[2]) for whole in wholes], pieces


def wide_scatter(groups, waits):
    count = lax.axis_size("wide")
    here = ring_place(lax.axis_index("wide"), count)
    directions = (1, -1)

    def part(partials, direction, back):
        device = ring_device((here - direction * back) & (count - 1), count)
        return jnp.concatenate(
            [
                lax.dynamic_index_in_dim(partial, place_of(device), 0, keepdims=False)
                for partial, place_of in partials
            ],
            -1,
        )

    moving = [part(g, d, 1).astype(BF16) for g, d in zip(groups, directions)]
    for hop in range(1, count):
        if hop in waits:
            moving = [after(m, *waits[hop]) for m in moving]
        came = lax.optimization_barrier(
            tuple(ring_step(m, d) for m, d in zip(moving, directions))
        )
        moving = [
            (c.astype(F32) + part(g, d, hop + 1).astype(F32)).astype(BF16)
            for c, g, d in zip(came, groups, directions)
        ]
    return moving


def wide_total(value):
    count = lax.axis_size("wide")
    bit = 1
    while bit < count:
        value = value + lax.ppermute(value, "wide", [(a, a ^ bit) for a in range(count)])
        bit *= 2
    return value


def turn_pairs(turn):
    wide, narrow = lax.axis_size("wide"), lax.axis_size("narrow")
    each = wide // narrow
    return [
        (each * b + h, narrow * h + (b + turn) % narrow)
        for b in range(narrow)
        for h in range(each)
    ]


def rows_to_blocks(shard, hops):
    wide, narrow = lax.axis_size("wide"), lax.axis_size("narrow")
    device, index = lax.axis_index("wide"), lax.axis_index("narrow")
    block = device >> ((wide // narrow).bit_length() - 1)
    rows = shard.shape[0] // narrow
    came = []
    for turn in range(narrow):
        start = ((block + turn) & (narrow - 1)) * rows
        leaving = lax.dynamic_slice_in_dim(shard, start, rows, 0)
        leaving = after(leaving, hops[1 if turn < narrow // 2 else 3])
        came.append(lax.ppermute(leaving, "wide", turn_pairs(turn)))
    came = [after(part, hops[-1]) for part in came]
    return [
        lax.select_n((device - (index ^ reverse_bits(p))) & (narrow - 1), *came)
        for p in range(narrow)
    ]


def blocks_to_rows(parts):
    wide, narrow = lax.axis_size("wide"), lax.axis_size("narrow")
    device, index = lax.axis_index("wide"), lax.axis_index("narrow")
    block = device >> ((wide // narrow).bit_length() - 1)
    came = []
    for turn in range(narrow):
        pairs = [(b, a) for a, b in turn_pairs(turn)]
        leaving = lax.select_n(
            reverse_bits(((device - turn) & (narrow - 1)) ^ index), *parts
        )
        came.append(lax.ppermute(leaving, "wide", pairs))
    return jnp.concatenate(
        [lax.select_n((k - block) & (narrow - 1), *came) for k in range(narrow)], 0
    )


def after(value, *others):
    return lax.optimization_barrier((value, *others))[0]


def scores_of(keys, query, starts, begin, extent):
    scores = dot(keys[0:extent, :], query * HEAD_DIM ** (-0.5), 1, 0)
    key_pos = lax.broadcasted_iota(jnp.int32, scores.shape, 0)
    query_pos = begin + lax.broadcasted_iota(jnp.int32, scores.shape, 1)
    return jnp.where((key_pos >= starts) & (key_pos <= query_pos), scores, MASKED)


def attend_kernel(query_ref, key_ref, value_ref, start_ref, out_ref, log_ref, keys):
    keys[...] = key_ref[...].T
    tokens = query_ref.shape[1]
    for begin in range(0, tokens, QUERY_BLOCK):
        extent = begin + QUERY_BLOCK
        span = slice(begin, extent)
        masked = scores_of(keys, query_ref[:, span], start_ref[:, span], begin, extent)
        top = jnp.max(masked, 0, keepdims=True)
        powers = jnp.exp(masked - top)
        total = jnp.sum(powers, 0, keepdims=True)
        log_total = top + jnp.log(total)
        probs = (powers * (1.0 / total)).astype(BF16)
        out_ref[:, span] = dot(value_ref[:, 0:extent], probs, 1, 0).astype(BF16)
        log_ref[0, :, span] = log_total


def attend(qkv, starts, first, heads):
    every, tokens = qkv.shape[0] // (3 * HEAD_DIM), qkv.shape[1]

    def piece(offset):
        return pl.BlockSpec((HEAD_DIM, tokens), lambda h: (offset * every + first + h, 0))

    return pl.pallas_call(
        attend_kernel,
        grid=(heads,),
        in_specs=[piece(0), piece(1), piece(2), pl.BlockSpec((1, tokens), lambda h: (0, 0))],
        out_specs=[
            pl.BlockSpec((HEAD_DIM, tokens), lambda h: (h, 0)),
            pl.BlockSpec((1, 1, tokens), lambda h: (h, 0, 0)),
        ],
        out_shape=[
            jax.ShapeDtypeStruct((heads * HEAD_DIM, tokens), BF16),
            jax.ShapeDtypeStruct((heads, 1, tokens), F32),
        ],
        scratch_shapes=[pltpu.VMEM((tokens, HEAD_DIM), BF16)],
        name="attend",
    )(qkv, qkv, qkv, starts)


def attend_back_kernel(
    query_ref, key_ref, value_ref, start_ref, log_ref, grad_ref, out_ref,
    back_ref, sums_ref, keys, values, grad_keys, grad_values,
):
    scale = HEAD_DIM ** (-0.5)
    keys[...] = key_ref[...].T
    values[...] = value_ref[...].T
    tokens = query_ref.shape[1]
    grad_keys[...] = jnp.zeros_like(grad_keys)
    grad_values[...] = jnp.zeros_like(grad_values)
    query_sum = jnp.zeros((HEAD_DIM, 1), F32)
    for begin in range(0, tokens, QUERY_BLOCK):
        extent = begin + QUERY_BLOCK
        span = slice(begin, extent)
        query = query_ref[:, span]
        grad = grad_ref[:, span]
        grad_b = grad.astype(BF16)
        delta = jnp.sum(grad * out_ref[:, span].astype(F32), 0, keepdims=True)
        masked = scores_of(keys, query, start_ref[:, span], begin, extent)
        probs = jnp.exp(masked - log_ref[0, :, span])
        grad_probs = dot(values[0:extent, :], grad_b, 1, 0)
        grad_scores = (probs * (grad_probs - delta)).astype(BF16)
        grad_query = dot(key_ref[:, 0:extent], grad_scores, 1, 0) * scale
        query_sum += jnp.sum(grad_query, 1, keepdims=True)
        back_ref[0, :, span] = grad_query.astype(BF16)
        grad_keys[:, 0:extent] += dot(query, grad_scores, 1, 1)
        grad_values[:, 0:extent] += dot(grad_b, probs.astype(BF16), 1, 1)
    grad_value = grad_values[...]
    back_ref[1] = (grad_keys[...] * scale).astype(BF16)
    back_ref[2] = grad_value.astype(BF16)
    sums_ref[0] = jnp.broadcast_to(query_sum, sums_ref.shape[1:])
    sums_ref[1] = jnp.broadcast_to(
        jnp.sum(grad_value, 1, keepdims=True), sums_ref.shape[1:]
    )


def attend_back(qkv, starts, log_total, grad_attended, attended):
    heads, tokens = qkv.shape[0] // (3 * HEAD_DIM), qkv.shape[1]

    def piece(offset):
        return pl.BlockSpec((HEAD_DIM, tokens), lambda h: (offset * heads + h, 0))

    back, sums = pl.pallas_call(
        attend_back_kernel,
        grid=(heads,),
        in_specs=[
            piece(0), piece(1), piece(2),
            pl.BlockSpec((1, tokens), lambda h: (0, 0)),
            pl.BlockSpec((1, 1, tokens), lambda h: (h, 0, 0)),
            piece(0), piece(0),
        ],
        out_specs=[
            pl.BlockSpec((3, HEAD_DIM, tokens), lambda h: (0, h, 0)),
            pl.BlockSpec((2, HEAD_DIM, 128), lambda h: (0, h, 0)),
        ],
        out_shape=[
            jax.ShapeDtypeStruct((3, heads * HEAD_DIM, tokens), BF16),
            jax.ShapeDtypeStruct((2, heads * HEAD_DIM, 128), F32),
        ],
        scratch_shapes=[
            pltpu.VMEM((tokens, HEAD_DIM), BF16),
            pltpu.VMEM((tokens, HEAD_DIM), BF16),
            pltpu.VMEM((HEAD_DIM, tokens), F32),
            pltpu.VMEM((HEAD_DIM, tokens), F32),
        ],
        name="attend_back",
    )(qkv, qkv, qkv, starts, log_total, grad_attended, attended)
    return back.reshape(3 * heads * HEAD_DIM, tokens), sums[:, :, 0]


def norm_stats(inputs):
    mean = jnp.sum(inputs, 0) / D
    variance = jnp.sum(inputs * inputs, 0) / D - mean * mean
    return mean, lax.rsqrt(variance + EPSILON)


def center(inputs, stats):
    return (inputs - stats[0][None]) * stats[1][None]


def norm_back_sums(grad_normed, centered, gain):
    weighted = grad_normed * gain[:, None]
    return jnp.stack([jnp.sum(weighted, 0), jnp.sum(weighted * centered, 0)])


def norm_back(grad_normed, centered, inv_std, gain, sums):
    return inv_std[None] * (
        grad_normed * gain[:, None] - sums[0][None] / D - centered * (sums[1][None] / D)
    )


def per_device(
    tokens,
    cotangent,
    segment_ids,
    ln1_gain,
    ln1_shift,
    w_query,
    w_key,
    w_value,
    bias_query,
    bias_value,
    w_out,
    bias_out,
    ln2_gain,
    ln2_shift,
    w_up,
    bias_up,
    w_down,
    bias_down,
):
    narrow, wide = lax.axis_size("narrow"), lax.axis_size("wide")
    index = lax.axis_index("narrow")
    feats, toks = tokens.shape
    shard_rows = w_query.shape[0]
    own_cols = (HEADS - 1) // narrow * HEAD_DIM
    head_cols = own_cols + HEAD_DIM
    last = (HEADS - 1) * HEAD_DIM

    qkv_pieces = narrow_pieces(jnp.concatenate([w_query, w_key, w_value], 0))
    token_pieces = narrow_pieces(tokens)
    inputs = jnp.concatenate(token_pieces, 0)
    vectors = [ln1_gain, ln1_shift, bias_out, ln2_gain, ln2_shift, bias_query, bias_value]
    small = narrow_pieces(jnp.concatenate(vectors))

    def vector(k, pieces):
        return jnp.concatenate([piece[k * feats : (k + 1) * feats] for piece in pieces])

    gain1, shift1, bias_o, gain2, shift2 = [vector(k, small) for k in range(5)]
    small_ordered = in_order(small)
    bias_q, bias_v = vector(5, small_ordered), vector(6, small_ordered)
    qkv_rows = jnp.concatenate(in_order(qkv_pieces), 1)

    def heads_of(array):
        own = lax.dynamic_slice_in_dim(array, index * own_cols, own_cols, array.ndim - 1)
        return jnp.concatenate([own, array[..., last:]], -1)

    head_rows = heads_of(qkv_rows)
    attention_shard = jnp.concatenate(
        [head_rows[k * shard_rows : (k + 1) * shard_rows] for k in range(3)] + [w_out], 1
    )

    (w_qkv, out_cols), hops = wide_gather(
        attention_shard,
        [(3 * head_cols, feature_place), (feats, lambda device: device)],
        {2: token_pieces[1:2], 3: (*token_pieces, *small)},
    )
    (up_cols,), up_hops = wide_gather(after(w_up, hops[5]), [(w_up.shape[1], feature_place)], {})
    down_shard = jnp.concatenate(
        narrow_exchange(rows_to_blocks(w_down, hops)), 1
    )
    down_block = lax.all_gather(down_shard, "wide", axis=0, tiled=True)
    cot_full = jnp.concatenate(narrow_pieces(after(cotangent, hops[1])), 0)
    out_pieces = narrow_pieces(out_cols)
    out_full = jnp.concatenate(out_pieces, 1)

    rows_f = inputs.astype(F32)
    stats1 = norm_stats(rows_f)
    centered1 = center(rows_f, stats1)
    normed1 = (centered1 * gain1[:, None] + shift1[:, None]).astype(BF16)
    bias_qkv = jnp.concatenate(
        [heads_of(bias_q), jnp.zeros((head_cols,), F32), heads_of(bias_v)]
    )
    qkv = (dot(w_qkv, normed1, 0, 0) + bias_qkv[:, None]).astype(BF16)
    starts = jnp.sum(
        (segment_ids[:, None] < segment_ids[None, :]).astype(jnp.int32), 0, keepdims=True
    )
    some = own_cols // HEAD_DIM // 2
    held = after(qkv, *up_hops[1:3])
    attended1, log1 = attend(held, starts, 0, some)
    held = after(held, attended1, out_pieces[1], down_shard, *up_hops[3:5])
    attended2, log2 = attend(held, starts, some, some)
    attended_own = jnp.concatenate([attended1, attended2], 0)
    attended_pieces = narrow_pieces(attended_own)
    attended3, log3 = attend(held, starts, 2 * some, 1)
    attended = jnp.concatenate([attended_own, attended3], 0)
    log_total = jnp.concatenate([log1, log2, log3], 0)
    attended_full = jnp.concatenate(in_order(attended_pieces) + [attended3], 0)
    resid = rows_f + dot(out_full, attended_full, 0, 0) + bias_o[:, None]

    stats2 = norm_stats(resid)
    centered2 = center(resid, stats2)
    normed2 = (centered2 * gain2[:, None] + shift2[:, None]).astype(BF16)
    hidden_pre = dot(up_cols, normed2, 0, 0) + bias_up[:, None]
    hidden, gelu_back = jax.vjp(gelu_tanh, hidden_pre)
    hidden = hidden.astype(BF16)
    grad_hidden = dot(down_block, cot_full, 1, 0)
    grad_pre = gelu_back(grad_hidden)[0]
    grad_pre_b = grad_pre.astype(BF16)
    grad_normed2 = dot(up_cols, grad_pre_b, 1, 0)
    sums2 = narrow_total(norm_back_sums(grad_normed2, centered2, gain2))
    stages2 = narrow_stages(grad_normed2)
    output_part = dot(down_block, after(hidden, stages2[1]), 0, 0)
    grad_normed2_own = after(stages2[-1], output_part)

    resid_own = resid[:feats]
    grad_up = dot(normed2, grad_pre_b, 1, 1).astype(BF16)
    grad_down = dot(hidden, cot_full, 1, 1).astype(BF16)
    grad_up = jnp.concatenate(
        in_order([grad_up[k * feats : (k + 1) * feats] for k in range(narrow)]), 0
    )
    sum_down = lax.psum_scatter(grad_down, "wide", scatter_dimension=0, tiled=True)
    grad_up = after(grad_up, grad_down)
    sum_up = lax.psum_scatter(grad_up, "wide", scatter_dimension=0, tiled=True)
    cot_own = cotangent.astype(F32)
    centered2_own = center(resid_own, stats2)
    grad_resid = cot_own + norm_back(
        grad_normed2_own, centered2_own, stats2[1], ln2_gain, sums2
    )
    grad_resid_own = grad_resid.astype(BF16)
    grad_resid_b = jnp.concatenate(narrow_pieces(grad_resid_own), 0)

    out_heads = jnp.concatenate(
        [lax.dynamic_slice_in_dim(out_full, index * own_cols, own_cols, 0), out_full[last:]], 0
    )
    grad_attended = dot(out_heads, grad_resid_b, 1, 0)
    sum_down = after(sum_down, grad_attended)
    down_parts = narrow_exchange(
        [sum_down[:, k * feats : (k + 1) * feats] for k in range(narrow)]
    )
    grad_qkv, head_sums = attend_back(qkv, starts, log_total, grad_attended, attended)
    grad_wout = dot(attended_full, after(grad_resid_own, grad_up), 1, 1).astype(BF16)
    output_sum = narrow_scatter(after(output_part, grad_qkv))
    output = (resid_own + (output_sum + bias_down[:, None])).astype(BF16)
    keep_last = (index == narrow - 1).astype(BF16)
    row_ids = jnp.arange(3 * head_cols) % head_cols
    counted = jnp.where(row_ids < own_cols, jnp.ones((), BF16), keep_last)
    grad_normed1 = dot(w_qkv, grad_qkv * counted[:, None], 1, 0)
    sums1 = narrow_total(norm_back_sums(grad_normed1, centered1, gain1))
    stages = narrow_stages(grad_normed1)
    grad_normed1_own = stages[-1]
    half = (3 * head_cols + feats) // 256 * 128 + 128
    grads = [
        dot(normed1, grad, 1, 1).astype(BF16).reshape(wide, shard_rows, -1)
        for grad in (grad_qkv[:half], grad_qkv[half:])
    ]
    grad_wout = grad_wout.reshape(wide, shard_rows, -1)
    waits = {2: stages[1], 6: stages[-1]}
    sum_down = blocks_to_rows(down_parts)
    sum_first, sum_rest = wide_scatter(
        [
            [(grads[0], feature_place)],
            [(grads[1], feature_place), (grad_wout, lambda device: device)],
        ],
        {2: (stages[1],), 4: down_parts[1:], 6: (stages[-1], sum_down)},
    )
    sum_qkv = jnp.concatenate([sum_first, sum_rest[:, :-feats]], -1)
    sum_wo = sum_rest[:, -feats:]
    sum_heads = jnp.concatenate(
        [sum_qkv[:, k * head_cols : (k + 1) * head_cols] for k in range(3)], 0
    )
    sum_cols = jnp.concatenate(
        in_order(narrow_pieces(sum_heads[:, :own_cols])) + [sum_heads[:, own_cols:]], 1
    )
    sum_own = lax.select_n(
        index, *[sum_cols[:, k * feats : (k + 1) * feats] for k in range(narrow)]
    ).astype(F32)

    centered1_own = center(tokens.astype(F32), stats1)
    grad_tokens = grad_resid + norm_back(
        grad_normed1_own, centered1_own, stats1[1], ln1_gain, sums1
    )

    placed = lax.dynamic_update_slice_in_dim(
        jnp.zeros((2, D), F32), head_sums[:, :own_cols], index * own_cols, 1
    )
    tail = jnp.where(index == narrow - 1, head_sums[:, own_cols:], 0.0)
    placed = lax.dynamic_update_slice_in_dim(placed, tail, last, 1)
    head_total = lax.dynamic_slice_in_dim(narrow_total(placed), index * feats, feats, 1)
    pieces = [
        jnp.sum(grad_normed1_own * centered1_own, 1),
        jnp.sum(grad_normed1_own, 1),
        head_total[0],
        head_total[1],
        jnp.sum(grad_resid, 1),
        jnp.sum(grad_normed2_own * centered2_own, 1),
        jnp.sum(grad_normed2_own, 1),
        jnp.sum(cot_own, 1),
        jnp.sum(grad_pre, 1),
    ]
    total = wide_total(jnp.concatenate(pieces))
    sums = [total[k * feats : (k + 1) * feats] for k in range(8)]
    return (
        output,
        grad_tokens,
        sums[0],
        sums[1],
        sum_own[:shard_rows],
        sum_own[shard_rows : 2 * shard_rows],
        sum_own[2 * shard_rows :],
        sums[2],
        sums[3],
        sum_wo.astype(F32),
        sums[4],
        sums[5],
        sums[6],
        sum_up.astype(F32),
        total[8 * feats :],
        sum_down.astype(F32),
        sums[7],
    )


def solution(mesh):
    matrix, vector = P("wide", "narrow"), P("narrow")
    acts = P("narrow", "wide")
    return jax.shard_map(
        per_device,
        mesh=mesh,
        in_specs=(
            acts, acts, P("wide"), vector, vector, matrix, matrix, matrix, vector, vector,
            matrix, vector, vector, vector, matrix, vector, matrix, vector,
        ),
        out_specs=(
            acts, acts, vector, vector, matrix, matrix, matrix, vector, vector,
            matrix, vector, vector, vector, matrix, vector, matrix, vector,
        ),
        check_vma=False,
    )
```
